128 devices in a mesh: seg: 32 (over z, y, x_lo), band: 4 (over x_hi, core).
Axes of the slice: x: 4 (x_hi: 2, x_lo: 2; x = x_hi * 2 + x_lo), y: 4, z: 4, core: 2. Of those that a mesh axis runs over, the one named last changes fastest.
Arguments:
- latents: bfloat16 [1024, 2560], P(('seg', 'band')), may hold values from -40 to 40
- weight_in: bfloat16 [3, 144, 384], replicated, may hold values from -0.3125 to 0.3125
- weight_mid: bfloat16 [3, 3456, 384], replicated, may hold values from -0.0625 to 0.0625
- weight_up: bfloat16 [3456, 192], replicated, may hold values from -0.109375 to 0.109375
- norm_gain: float32 [384], replicated, may hold values from 0.5 to 1.5
- norm_shift: float32 [384], replicated, may hold values from -2.5 to 2.5
Outputs:
- decoded: bfloat16 [64, 32, 61440], P('seg', 'band')
The draws below stay inside these ranges and needn't reach their ends.
All inputs are finite; a program needn't handle non-finite values.
Results may differ from the reference program's by a relative error of at most 0.012.
Values may be sent and summed in bfloat16 or wider, within the bound.
A program may use at most 128 MiB of HBM per device.

```python
import jax
import jax.numpy as jnp
from jax import lax

C_LAT = 16
C_MID = 384
C_OUT = 192
GROUPS = 32
COLS = 160
HL = 16
FRAMES = 64


def draw_latents(key, part):
    key_base, key_rows, key_cols = jax.random.split(key, 3)
    row_ids = (jnp.arange(FRAMES * HL, dtype=jnp.int32) % HL).astype(jnp.float32)
    row_frac = row_ids / max(HL - 1, 1)
    row_jitter = jnp.exp(jax.random.uniform(key_rows, (FRAMES * HL,), jnp.float32, jnp.log(0.6), jnp.log(1.7)))
    col_scale = jnp.exp(jax.random.uniform(key_cols, (COLS,), jnp.float32, jnp.log(0.32), jnp.log(3.2)))
    base_value = jnp.clip(jax.random.normal(key_base, (FRAMES * HL, COLS, C_LAT), jnp.float32), -4.0, 4.0)
    row_ramp = 0.55 * jnp.exp(jnp.log(3.0) * row_frac)
    scaled = base_value * (row_ramp * row_jitter)[:, None, None] * col_scale[None, :, None]
    return scaled.reshape(FRAMES * HL, COLS * C_LAT).astype(jnp.bfloat16)


def scatter_about(rng, dims, scale, limit, kind=jnp.bfloat16):
    values = scale * jax.random.normal(rng, dims, jnp.float32)
    return jnp.clip(values, min=-limit, max=limit).astype(kind)


def setup_inputs(seed: int = 0) -> dict:
    streams_of = jax.random.split(jax.random.key(seed), 7)
    return {
        "latents": draw_latents(jax.random.fold_in(streams_of[6], 71), 0),
        "weight_in": scatter_about(streams_of[1], (3, 9 * C_LAT, C_MID), (27 * C_LAT) ** -0.5, 0.3125),
        "weight_mid": scatter_about(streams_of[2], (3, 9 * C_MID, C_MID), (27 * C_MID) ** -0.5, 0.0625),
        "weight_up": scatter_about(streams_of[3], (9 * C_MID, C_OUT), (9 * C_MID) ** -0.5, 0.109375),
        "norm_gain": jnp.clip(jax.random.uniform(streams_of[4], (C_MID,), jnp.float32, 0.5, 1.5), 0.5, 1.5),
        "norm_shift": scatter_about(streams_of[5], (C_MID,), 0.5, 2.5, jnp.float32),
    }


def stack_taps(padded, rows_out, columns):
    pieces = [padded[:, row_shift:row_shift + rows_out, col_shift:col_shift + columns, :] for row_shift in range(3) for col_shift in range(3)]
    return jnp.concatenate(pieces, axis=-1)

def causal_conv(source, weight, frames_out, rows_out):
    columns = source.shape[2]
    padded = jnp.pad(source, ((0, 0), (0, 0), (1, 1), (0, 0)))
    tap_stack = stack_taps(padded, rows_out, columns)
    tap_width = tap_stack.shape[-1]
    accumulated = jnp.zeros((frames_out * rows_out * columns, weight.shape[-1]), jnp.float32)
    for tap_index in range(3):
        tap_rows = tap_stack[tap_index:tap_index + frames_out].reshape(frames_out * rows_out * columns, tap_width)
        accumulated = accumulated + jnp.dot(tap_rows, weight[tap_index], preferred_element_type=jnp.float32)
    return accumulated.reshape(frames_out, rows_out, columns, weight.shape[-1])

def group_sums(values, groups):
    frames = values.shape[0]
    grouped = values.astype(jnp.float32).reshape(frames, -1, groups, values.shape[-1] // groups)
    return (lax.optimization_barrier(jnp.sum(grouped, axis=(1, 3))), lax.optimization_barrier(jnp.sum(grouped * grouped, axis=(1, 3))))

def activate(values, mean_value, inv_std, norm_gain, norm_shift, groups):
    frames, rows_here, columns, channels = values.shape
    grouped = values.astype(jnp.float32).reshape(frames, rows_here, columns, groups, channels // groups)
    normed = (grouped - mean_value[:, None, None, :, None]) * inv_std[:, None, None, :, None]
    normed = normed.reshape(values.shape) * norm_gain + norm_shift
    return jax.nn.silu(normed).astype(jnp.bfloat16)

def conv_video(latent_video, weight):
    padded = jnp.pad(latent_video, ((2, 0), (1, 1), (0, 0), (0, 0)))

    def one_frame(frame_index):
        window = lax.dynamic_slice_in_dim(padded, frame_index.astype(jnp.int32), 3, 0)
        return causal_conv(window, weight, 1, HL)[0]
    return lax.map(one_frame, jnp.arange(FRAMES, dtype=jnp.int32))

def reference(latents, weight_in, weight_mid, weight_up, norm_gain, norm_shift):
    latent_video = latents.reshape(FRAMES, HL, COLS, C_LAT)
    coarse = conv_video(latent_video, weight_in).astype(jnp.bfloat16)
    cell_count = HL * COLS * (C_MID // GROUPS)
    sum_one, sum_two = group_sums(coarse, GROUPS)
    mean_value = sum_one / cell_count
    inv_std = lax.rsqrt(sum_two / cell_count - mean_value * mean_value + 1e-06)
    active = activate(coarse, mean_value, inv_std, norm_gain, norm_shift, GROUPS)
    refined = (coarse.astype(jnp.float32) + conv_video(active, weight_mid)).astype(jnp.bfloat16)

    def upsample_frame(frame):
        doubled = jnp.repeat(jnp.repeat(frame, 2, axis=0), 2, axis=1)
        padded = jnp.pad(doubled, ((1, 1), (1, 1), (0, 0)))
        tap_stack = stack_taps(padded[None], 2 * HL, 2 * COLS)[0]
        result = jnp.dot(tap_stack.reshape(-1, tap_stack.shape[-1]), weight_up, preferred_element_type=jnp.float32)
        return result.reshape(2 * HL, 2 * COLS * C_OUT).astype(jnp.bfloat16)
    return lax.map(upsample_frame, refined)
```

```python
import functools

import jax
import jax.numpy as jnp
from jax import lax
from jax.experimental import pallas as pl
from jax.experimental.pallas import tpu as pltpu
from jax.sharding import PartitionSpec as P

C_LAT = 16
C_MID = 384
C_OUT = 192
GROUPS = 32
COLS = 160
HL = 16
FR = 2
RB = 4
BANDS = 4
CELLS = HL * COLS * (C_MID // GROUPS)
TAPW = 3 * C_MID
PAIRS = ((1, 2), (3, 4), (0, 5))
MESH = pl.DeviceIdType.MESH
BF = jnp.bfloat16
F32 = jnp.float32


def col_shifts(v):
    cols = v.shape[0]
    j = lax.broadcasted_iota(jnp.int32, v.shape, 0)
    before = jnp.where(j == 0, 0.0, pltpu.roll(v, 1, 0))
    after = jnp.where(j == cols - 1, 0.0, pltpu.roll(v, cols - 1, 0))
    return before, v, after


def features_kernel(
    segs, z, w_in, w_mid, w_upt, gain, shift, x1_out, u_out,
    lrecv, lst, wb, x0s, wm, gs, st_src, st_recv, v3, x1s,
    wsem, lsend_sem, lrecv_sem, ssend_sem, srecv_sem, hsend_sem, hrecv_sem,
):
    s = lax.axis_index("seg")
    b = lax.axis_index("band")
    half = lax.rem(b, 2)

    load_w = pltpu.make_async_copy(w_mid, wm, wsem)
    load_w.start()

    barrier = pltpu.get_barrier_semaphore()

    def each_peer(fn):
        for ds in range(-2, 3):
            for tb in range(BANDS):
                ok = jnp.logical_and(s + ds >= 0, s + ds < segs)
                if ds == 0:
                    ok = jnp.logical_and(ok, b != tb)
                pl.when(ok)(functools.partial(fn, ds, tb))

    def greet(ds, tb):
        pl.semaphore_signal(barrier, inc=1, device_id={"seg": s + ds, "band": jnp.int32(tb)}, device_id_type=MESH)

    peers = -1
    for ds in range(-2, 3):
        ok = jnp.logical_and(s + ds >= 0, s + ds < segs)
        peers = peers + jnp.where(ok, BANDS, 0)

    each_peer(greet)

    for q, pair in enumerate(PAIRS):
        for k, r in enumerate(pair):
            for t in range(3):
                for dx in range(3):
                    for rw in range(8):
                        dy = rw - r
                        at = t * 384 + dx * 128 + rw * 16
                        if 0 <= dy < 3:
                            blk = w_in[t, (dy * 3 + dx) * 16 : (dy * 3 + dx + 1) * 16, :]
                        else:
                            blk = jnp.zeros((16, C_MID), BF)
                        wb[q, at : at + 16, k * C_MID : (k + 1) * C_MID] = blk

    pl.semaphore_wait(barrier, peers)

    def latent_copy(ds, tb):
        return pltpu.make_async_remote_copy(
            src_ref=z,
            dst_ref=lrecv.at[8 - 4 * ds + b],
            send_sem=lsend_sem.at[ds * BANDS + tb],
            recv_sem=lrecv_sem.at[8 - 4 * ds + b],
            device_id={"seg": s + ds, "band": jnp.int32(tb)},
            device_id_type=MESH,
        )

    def each_latent_copy(fn):
        for ds in range(3):
            for tb in range(BANDS):
                ok = s + ds < segs
                if tb == 0:
                    ok = jnp.logical_and(ok, half == 0)
                if tb == BANDS - 1:
                    ok = jnp.logical_and(ok, half == 1)
                if ds == 0:
                    ok = jnp.logical_and(ok, b != tb)
                pl.when(ok)(functools.partial(fn, ds, tb))

    each_latent_copy(lambda ds, tb: latent_copy(ds, tb).start())
    lrecv[8 + b] = z[...]

    sets = (((0,), (1, 2)), ((0, 1), (2,)))
    for r2 in range(2):
        for c2 in range(2):
            ph = r2 * 2 + c2
            for rt in range(2):
                for ct in range(2):
                    acc = None
                    for dy in sets[r2][rt]:
                        for dx in sets[c2][ct]:
                            w = w_upt[:, (dy * 3 + dx) * C_MID : (dy * 3 + dx + 1) * C_MID].astype(F32)
                            acc = w if acc is None else acc + w
                    k0 = (rt * 2 + ct) * C_MID
                    n0 = 64 * c2
                    u_out[ph, n0 : n0 + C_OUT, k0 : k0 + C_MID] = acc.astype(BF)
            z0 = C_OUT if c2 == 0 else 0
            u_out[ph, z0 : z0 + 64, :] = jnp.zeros((64, 4 * C_MID), BF)

    load_w.wait()

    def combine(i, c):
        rows = pl.ds(pl.multiple_of(i * 128, 128), 128)
        w0, w1, w2 = (wm[t, rows, :].astype(F32) for t in range(3))
        outer, mid = (w0 + w2) * 0.5, w1 * 0.5
        gs[0, rows, :] = (outer + mid).astype(BF)
        gs[1, rows, :] = (outer - mid).astype(BF)
        return c

    lax.fori_loop(0, 27, combine, 0)

    def arrived(slot):
        pltpu.make_async_remote_copy(
            src_ref=z,
            dst_ref=lrecv.at[slot],
            send_sem=lsend_sem.at[0],
            recv_sem=lrecv_sem.at[slot],
            device_id={"seg": s, "band": b},
            device_id_type=MESH,
        ).wait_recv()

    for slot in range(12):
        ok = s - 2 + slot // 4 >= 0
        if slot % 2 == 0:
            ok = jnp.logical_and(ok, b <= 2)
        else:
            ok = jnp.logical_and(ok, b >= 1)
        if slot >= 8:
            ok = jnp.logical_and(ok, b != slot - 8)
        pl.when(ok)(functools.partial(arrived, slot))

    lane = lax.broadcasted_iota(jnp.int32, (COLS, 128), 1)
    row = 4 * b - 2 + lane // 16
    in_frame = jnp.logical_and(row >= 0, row < HL)
    for g in range(6):
        both = jnp.concatenate([lrecv[2 * g].astype(F32), lrecv[2 * g + 1].astype(F32)], axis=1)
        win = pltpu.roll(both, lax.rem(32 - 64 * b + 256, 256), 1)[:, :128]
        win = jnp.where(jnp.logical_and(in_frame, 2 * s - 4 + g >= 0), win, 0.0)
        taps = jnp.concatenate(col_shifts(win), axis=1).astype(BF)
        for f in range(4):
            t = g - f
            if 0 <= t < 3:
                lst[f * COLS : (f + 1) * COLS, t * 384 : (t + 1) * 384] = taps

    def conv_in(q):
        return jnp.dot(lst[...], wb[q], preferred_element_type=F32).astype(BF)

    sums = [[None] * 4, [None] * 4]
    for q, pair in enumerate(PAIRS[:2]):
        x0 = conv_in(q)
        for f in range(4):
            for k, r in enumerate(pair):
                part = x0[f * COLS : (f + 1) * COLS, k * C_MID : (k + 1) * C_MID]
                x0s[f, r] = part
                wide = part.astype(F32)
                for m, v in enumerate((wide, wide * wide)):
                    tot = jnp.sum(v, axis=0, keepdims=True)
                    sums[m][f] = tot if sums[m][f] is None else sums[m][f] + tot
    st_src[...] = jnp.concatenate(sums[0] + sums[1], axis=0)

    def stat_copy(tb):
        return pltpu.make_async_remote_copy(
            src_ref=st_src,
            dst_ref=st_recv.at[b],
            send_sem=ssend_sem.at[tb],
            recv_sem=srecv_sem.at[b],
            device_id={"seg": s, "band": jnp.int32(tb)},
            device_id_type=MESH,
        )

    for tb in range(BANDS):
        pl.when(b != tb)(lambda tb=tb: stat_copy(tb).start())
    st_recv[b] = st_src[...]

    x0 = conv_in(2)
    for f in range(4):
        for k, r in enumerate(PAIRS[2]):
            x0s[f, r] = x0[f * COLS : (f + 1) * COLS, k * C_MID : (k + 1) * C_MID]

    def stats_in(ob):
        pltpu.make_async_remote_copy(
            src_ref=st_src,
            dst_ref=st_recv.at[ob],
            send_sem=ssend_sem.at[0],
            recv_sem=srecv_sem.at[ob],
            device_id={"seg": s, "band": b},
            device_id_type=MESH,
        ).wait_recv()

    for ob in range(BANDS):
        pl.when(b != ob)(functools.partial(stats_in, ob))

    total = (st_recv[0] + st_recv[1]) + (st_recv[2] + st_recv[3])
    per = C_MID // GROUPS
    gi = lax.broadcasted_iota(jnp.int32, (C_MID, C_MID), 0) // per
    gj = lax.broadcasted_iota(jnp.int32, (C_MID, C_MID), 1) // per
    same = jnp.where(gi == gj, 1.0, 0.0).astype(F32)
    total = jnp.dot(total, same, preferred_element_type=F32, precision=lax.Precision.HIGHEST)
    mean = total[0:4] / CELLS
    rstd = lax.rsqrt(total[4:8] / CELLS - mean * mean + 1e-6)
    mul = rstd * gain[...].reshape(1, C_MID)
    add = shift[...].reshape(1, C_MID) - mean * mul

    def activate(r, c):
        arow = 4 * b - 1 + r
        row_ok = jnp.logical_and(arow >= 0, arow < HL)
        a = []
        for f in range(4):
            ok = jnp.logical_and(row_ok, 2 * s - 2 + f >= 0)
            v = x0s[f, r].astype(F32) * mul[f : f + 1] + add[f : f + 1]
            hv = 0.5 * v
            act = hv + hv * jnp.tanh(hv)
            a.append(jnp.where(ok, act, 0.0))
        for i, v in enumerate((a[0] - a[2], a[1] + a[2], a[2] - a[1], a[1] - a[3])):
            for dx, w in enumerate(col_shifts(v)):
                v3[i, r, :, dx * C_MID : (dx + 1) * C_MID] = w.astype(BF)
        return c

    lax.fori_loop(0, 6, activate, 0)

    def halo_copy(up):
        return pltpu.make_async_remote_copy(
            src_ref=x1s.at[:, 1 if up else RB],
            dst_ref=x1s.at[:, RB + 1 if up else 0],
            send_sem=hsend_sem.at[0 if up else 1],
            recv_sem=hrecv_sem.at[0 if up else 1],
            device_id={"seg": s, "band": b - 1 if up else b + 1},
            device_id_type=MESH,
        )

    def residual(h, c):
        ra, rb = h, 3 - h

        def product(i):
            acc = None
            for dy in range(3):
                x = jnp.concatenate([v3[i, ra + dy], v3[i, rb + dy]], axis=0)
                ks = slice(dy * TAPW, (dy + 1) * TAPW)
                g = (wm[0, ks, :], gs[0, ks, :], gs[1, ks, :], wm[2, ks, :])[i]
                d = jnp.dot(x, g, preferred_element_type=F32)
                acc = d if acc is None else acc + d
            return acc

        t1, t2, t3, t4 = (product(i) for i in range(4))
        for f, y in enumerate((t1 + t2 + t3, t2 - t3 - t4)):
            x1s[f, 1 + ra] = (x0s[FR + f, 1 + ra].astype(F32) + y[:COLS]).astype(BF)
            x1s[f, 1 + rb] = (x0s[FR + f, 1 + rb].astype(F32) + y[COLS:]).astype(BF)

        @pl.when(h == 0)
        def _():
            pl.when(b > 0)(lambda: halo_copy(True).start())
            pl.when(b < BANDS - 1)(lambda: halo_copy(False).start())

        return c

    lax.fori_loop(0, 2, residual, 0)

    @pl.when(b > 0)
    def _():
        halo_copy(False).wait_recv()

    @pl.when(b < BANDS - 1)
    def _():
        halo_copy(True).wait_recv()

    x1_out[:, 1 : RB + 1] = x1s[:, 1 : RB + 1]
    nothing = jnp.zeros((FR, COLS, C_MID), BF)
    x1_out[:, 0] = jnp.where(b > 0, x1s[:, 0], nothing)
    x1_out[:, RB + 1] = jnp.where(b < BANDS - 1, x1s[:, RB + 1], nothing)

    pl.when(b > 0)(lambda: halo_copy(True).wait_send())
    pl.when(b < BANDS - 1)(lambda: halo_copy(False).wait_send())
    each_latent_copy(lambda ds, tb: latent_copy(ds, tb).wait_send())
    for tb in range(BANDS):
        pl.when(b != tb)(lambda tb=tb: stat_copy(tb).wait_send())


def upsample_kernel(x1, u, out, x3, zs):
    def widen(r, c):
        v = x1[0, r].astype(F32)
        for dx, w in enumerate(col_shifts(v)):
            x3[r, :, dx * C_MID : (dx + 1) * C_MID] = w.astype(BF)
        return c

    lax.fori_loop(0, RB + 2, widen, 0)
    for r2 in range(2):
        y = []
        for c2 in range(2):
            acc = None
            for rt in range(2):
                x = x3[r2 + rt : r2 + rt + RB, :, c2 * C_MID : (c2 + 2) * C_MID].reshape(RB * COLS, 2 * C_MID)
                d = lax.dot_general(
                    x, u[r2 * 2 + c2, :, rt * 2 * C_MID : (rt + 1) * 2 * C_MID],
                    (((1,), (1,)), ((), ())), preferred_element_type=F32,
                )
                acc = d if acc is None else acc + d
            y.append(acc)
        full = jnp.concatenate([y[0][:, :128], y[0][:, 128:] + y[1][:, :128], y[1][:, 128:]], axis=1)
        for p in range(RB):
            for l in range(3):
                zs[l, pl.ds(2 * p + r2, COLS, stride=8), :] = full[p * COLS : (p + 1) * COLS, l * 128 : (l + 1) * 128]

    for q in range(COLS):
        for l in range(3):
            at = q * 2 * C_OUT + l * 128
            out[0, :, at : at + 128] = zs[l, q * 8 : (q + 1) * 8, :].astype(BF)


def local(segs, latents, weight_in, weight_mid, weight_up, norm_gain, norm_shift):
    z = latents.reshape(8, COLS, C_LAT).transpose(1, 0, 2).reshape(COLS, 8 * C_LAT)
    vm = pl.BlockSpec(memory_space=pltpu.VMEM)
    x1, u = pl.pallas_call(
        functools.partial(features_kernel, segs),
        out_shape=(
            jax.ShapeDtypeStruct((FR, RB + 2, COLS, C_MID), BF),
            jax.ShapeDtypeStruct((4, 256, 4 * C_MID), BF),
        ),
        in_specs=[vm, vm, pl.BlockSpec(memory_space=pl.ANY), vm, vm, vm],
        out_specs=(vm, vm),
        scratch_shapes=[
            pltpu.VMEM((12, COLS, 128), BF),
            pltpu.VMEM((4 * COLS, 3 * 384), BF),
            pltpu.VMEM((3, 3 * 384, 2 * C_MID), BF),
            pltpu.VMEM((4, RB + 2, COLS, C_MID), BF),
            pltpu.VMEM((3, 9 * C_MID, C_MID), BF),
            pltpu.VMEM((2, 9 * C_MID, C_MID), BF),
            pltpu.VMEM((8, C_MID), F32),
            pltpu.VMEM((BANDS, 8, C_MID), F32),
            pltpu.VMEM((4, RB + 2, COLS, TAPW), BF),
            pltpu.VMEM((FR, RB + 2, COLS, C_MID), BF),
            pltpu.SemaphoreType.DMA,
            pltpu.SemaphoreType.DMA((12,)),
            pltpu.SemaphoreType.DMA((12,)),
            pltpu.SemaphoreType.DMA((BANDS,)),
            pltpu.SemaphoreType.DMA((BANDS,)),
            pltpu.SemaphoreType.DMA((2,)),
            pltpu.SemaphoreType.DMA((2,)),
        ],
        compiler_params=pltpu.CompilerParams(collective_id=0, has_side_effects=True, vmem_limit_bytes=56 << 20),
        name="features",
    )(z, weight_in, weight_mid, weight_up.T, norm_gain, norm_shift)
    return pl.pallas_call(
        upsample_kernel,
        grid=(FR,),
        out_shape=jax.ShapeDtypeStruct((FR, 2 * RB, 2 * COLS * C_OUT), BF),
        in_specs=[
            pl.BlockSpec((1, RB + 2, COLS, C_MID), lambda f: (f, 0, 0, 0)),
            pl.BlockSpec((4, 256, 4 * C_MID), lambda f: (0, 0, 0)),
        ],
        out_specs=pl.BlockSpec((1, 2 * RB, 2 * COLS * C_OUT), lambda f: (f, 0, 0)),
        scratch_shapes=[
            pltpu.VMEM((RB + 2, COLS, TAPW), BF),
            pltpu.VMEM((3, COLS * 8, 128), F32),
        ],
        compiler_params=pltpu.CompilerParams(vmem_limit_bytes=40 << 20),
        name="upsample",
    )(x1, u)


def solution(mesh):
    return jax.shard_map(
        functools.partial(local, mesh.shape["seg"]),
        mesh=mesh,
        in_specs=(P(("seg", "band"), None), P(), P(), P(), P(), P()),
        out_specs=P("seg", "band", None),
        check_vma=False,
    )
```

```python
import functools

import jax
import jax.numpy as jnp
from jax import lax
from jax.experimental import pallas as pl
from jax.experimental.pallas import tpu as pltpu
from jax.sharding import PartitionSpec as P

C_LAT = 16
C_MID = 384
C_OUT = 192
GROUPS = 32
COLS = 160
HL = 16
FR = 2
RB = 4
BANDS = 4
CELLS = HL * COLS * (C_MID // GROUPS)
TAPW = 3 * C_MID
PAIRS = ((1, 2), (3, 4), (0, 5))
MESH = pl.DeviceIdType.MESH
BF = jnp.bfloat16
F32 = jnp.float32


def col_shifts(v):
    cols = v.shape[0]
    j = lax.broadcasted_iota(jnp.int32, v.shape, 0)
    before = jnp.where(j == 0, 0.0, pltpu.roll(v, 1, 0))
    after = jnp.where(j == cols - 1, 0.0, pltpu.roll(v, cols - 1, 0))
    return before, v, after


def columns_first(lat):
    blocks = COLS * C_LAT // 128
    x = jnp.concatenate([lat[:, k * 128 : (k + 1) * 128].astype(F32)[None] for k in range(blocks)], axis=0)
    row = lax.broadcasted_iota(jnp.int32, x.shape, 1)
    col = lax.broadcasted_iota(jnp.int32, x.shape, 2) // C_LAT
    for k in (1, 2, 4):
        r, c = (row // k) % 2, (col // k) % 2
        from_below = pltpu.roll(pltpu.roll(x, k * C_LAT, 2), 8 - k, 1)
        from_above = pltpu.roll(pltpu.roll(x, 128 - k * C_LAT, 2), k, 1)
        x = jnp.where(r == c, x, jnp.where(r < c, from_below, from_above))
    return x.reshape(COLS, 128).astype(BF)


def decoder_kernel(
    segs, lat_hbm, w_in_hbm, w_mid, w_up_hbm, gain_hbm, shift_hbm, out,
    lat, gain, shift, w_in, w_upt, z, lrecv, lst, wb, x0s, wm, gs, st_src, st_recv, v3, x1s, u, x3, zs,
    wsem, lsend_sem, lrecv_sem, ssend_sem, srecv_sem, hsend_sem, hrecv_sem,
):
    s = lax.axis_index("seg")
    b = lax.axis_index("band")
    half = lax.rem(b, 2)

    load_in = pltpu.make_async_copy(w_in_hbm, w_in, wsem.at[0])
    load_up = pltpu.make_async_copy(w_up_hbm, w_upt, wsem.at[1])
    load_w = pltpu.make_async_copy(w_mid, wm, wsem.at[2])
    load_lat = pltpu.make_async_copy(lat_hbm, lat, wsem.at[3])
    load_gain = pltpu.make_async_copy(gain_hbm, gain, wsem.at[4])
    load_shift = pltpu.make_async_copy(shift_hbm, shift, wsem.at[5])
    for load in (load_lat, load_in, load_up, load_w, load_gain, load_shift):
        load.start()

    barrier = pltpu.get_barrier_semaphore()

    def each_peer(fn):
        for ds in range(-2, 3):
            for tb in range(BANDS):
                ok = jnp.logical_and(s + ds >= 0, s + ds < segs)
                if ds == 0:
                    ok = jnp.logical_and(ok, b != tb)
                pl.when(ok)(functools.partial(fn, ds, tb))

    def greet(ds, tb):
        pl.semaphore_signal(barrier, inc=1, device_id={"seg": s + ds, "band": jnp.int32(tb)}, device_id_type=MESH)

    peers = -1
    for ds in range(-2, 3):
        ok = jnp.logical_and(s + ds >= 0, s + ds < segs)
        peers = peers + jnp.where(ok, BANDS, 0)

    each_peer(greet)
    load_lat.wait()
    z[...] = columns_first(lat)

    load_in.wait()
    for q, pair in enumerate(PAIRS):
        for k, r in enumerate(pair):
            for t in range(3):
                for dx in range(3):
                    for rw in range(8):
                        dy = rw - r
                        at = t * 384 + dx * 128 + rw * 16
                        if 0 <= dy < 3:
                            blk = w_in[t, (dy * 3 + dx) * 16 : (dy * 3 + dx + 1) * 16, :]
                        else:
                            blk = jnp.zeros((16, C_MID), BF)
                        wb[q, at : at + 16, k * C_MID : (k + 1) * C_MID] = blk

    pl.semaphore_wait(barrier, peers)

    def latent_copy(ds, tb):
        return pltpu.make_async_remote_copy(
            src_ref=z,
            dst_ref=lrecv.at[8 - 4 * ds + b],
            send_sem=lsend_sem.at[ds * BANDS + tb],
            recv_sem=lrecv_sem.at[8 - 4 * ds + b],
            device_id={"seg": s + ds, "band": jnp.int32(tb)},
            device_id_type=MESH,
        )

    def each_latent_copy(fn):
        for ds in range(3):
            for tb in range(BANDS):
                ok = s + ds < segs
                if tb == 0:
                    ok = jnp.logical_and(ok, half == 0)
                if tb == BANDS - 1:
                    ok = jnp.logical_and(ok, half == 1)
                if ds == 0:
                    ok = jnp.logical_and(ok, b != tb)
                pl.when(ok)(functools.partial(fn, ds, tb))

    each_latent_copy(lambda ds, tb: latent_copy(ds, tb).start())
    lrecv[8 + b] = z[...]

    load_up.wait()
    sets = (((0,), (1, 2)), ((0, 1), (2,)))
    for r2 in range(2):
        for c2 in range(2):
            ph = r2 * 2 + c2
            for rt in range(2):
                for ct in range(2):
                    acc = None
                    for dy in sets[r2][rt]:
                        for dx in sets[c2][ct]:
                            w = w_upt[:, (dy * 3 + dx) * C_MID : (dy * 3 + dx + 1) * C_MID].astype(F32)
                            acc = w if acc is None else acc + w
                    k0 = (rt * 2 + ct) * C_MID
                    n0 = 64 * c2
                    u[ph, n0 : n0 + C_OUT, k0 : k0 + C_MID] = acc.astype(BF)
            z0 = C_OUT if c2 == 0 else 0
            u[ph, z0 : z0 + 64, :] = jnp.zeros((64, 4 * C_MID), BF)

    load_w.wait()

    def combine(i, c):
        rows = pl.ds(pl.multiple_of(i * 128, 128), 128)
        w0, w1, w2 = (wm[t, rows, :].astype(F32) for t in range(3))
        outer, mid = (w0 + w2) * 0.5, w1 * 0.5
        gs[0, rows, :] = (outer + mid).astype(BF)
        gs[1, rows, :] = (outer - mid).astype(BF)
        return c

    lax.fori_loop(0, 27, combine, 0)

    def arrived(slot):
        pltpu.make_async_remote_copy(
            src_ref=z,
            dst_ref=lrecv.at[slot],
            send_sem=lsend_sem.at[0],
            recv_sem=lrecv_sem.at[slot],
            device_id={"seg": s, "band": b},
            device_id_type=MESH,
        ).wait_recv()

    for slot in range(12):
        ok = s - 2 + slot // 4 >= 0
        if slot % 2 == 0:
            ok = jnp.logical_and(ok, b <= 2)
        else:
            ok = jnp.logical_and(ok, b >= 1)
        if slot >= 8:
            ok = jnp.logical_and(ok, b != slot - 8)
        pl.when(ok)(functools.partial(arrived, slot))

    lane = lax.broadcasted_iota(jnp.int32, (COLS, 128), 1)
    row = 4 * b - 2 + lane // 16
    in_frame = jnp.logical_and(row >= 0, row < HL)
    for g in range(6):
        both = jnp.concatenate([lrecv[2 * g].astype(F32), lrecv[2 * g + 1].astype(F32)], axis=1)
        win = pltpu.roll(both, lax.rem(32 - 64 * b + 256, 256), 1)[:, :128]
        win = jnp.where(jnp.logical_and(in_frame, 2 * s - 4 + g >= 0), win, 0.0)
        taps = jnp.concatenate(col_shifts(win), axis=1).astype(BF)
        for f in range(4):
            t = g - f
            if 0 <= t < 3:
                lst[f * COLS : (f + 1) * COLS, t * 384 : (t + 1) * 384] = taps

    def conv_in(q):
        return jnp.dot(lst[...], wb[q], preferred_element_type=F32).astype(BF)

    sums = [[None] * 4, [None] * 4]
    for q, pair in enumerate(PAIRS[:2]):
        x0 = conv_in(q)
        for f in range(4):
            for k, r in enumerate(pair):
                part = x0[f * COLS : (f + 1) * COLS, k * C_MID : (k + 1) * C_MID]
                x0s[f, r] = part
                wide = part.astype(F32)
                for m, v in enumerate((wide, wide * wide)):
                    tot = jnp.sum(v, axis=0, keepdims=True)
                    sums[m][f] = tot if sums[m][f] is None else sums[m][f] + tot
    st_src[...] = jnp.concatenate(sums[0] + sums[1], axis=0)

    def stat_copy(tb):
        return pltpu.make_async_remote_copy(
            src_ref=st_src,
            dst_ref=st_recv.at[b],
            send_sem=ssend_sem.at[tb],
            recv_sem=srecv_sem.at[b],
            device_id={"seg": s, "band": jnp.int32(tb)},
            device_id_type=MESH,
        )

    for tb in range(BANDS):
        pl.when(b != tb)(lambda tb=tb: stat_copy(tb).start())
    st_recv[b] = st_src[...]

    x0 = conv_in(2)
    for f in range(4):
        for k, r in enumerate(PAIRS[2]):
            x0s[f, r] = x0[f * COLS : (f + 1) * COLS, k * C_MID : (k + 1) * C_MID]

    def stats_in(ob):
        pltpu.make_async_remote_copy(
            src_ref=st_src,
            dst_ref=st_recv.at[ob],
            send_sem=ssend_sem.at[0],
            recv_sem=srecv_sem.at[ob],
            device_id={"seg": s, "band": b},
            device_id_type=MESH,
        ).wait_recv()

    for ob in range(BANDS):
        pl.when(b != ob)(functools.partial(stats_in, ob))

    total = (st_recv[0] + st_recv[1]) + (st_recv[2] + st_recv[3])
    per = C_MID // GROUPS
    gi = lax.broadcasted_iota(jnp.int32, (C_MID, C_MID), 0) // per
    gj = lax.broadcasted_iota(jnp.int32, (C_MID, C_MID), 1) // per
    same = jnp.where(gi == gj, 1.0, 0.0).astype(F32)
    total = jnp.dot(total, same, preferred_element_type=F32, precision=lax.Precision.HIGHEST)
    mean = total[0:4] / CELLS
    rstd = lax.rsqrt(total[4:8] / CELLS - mean * mean + 1e-6)
    load_gain.wait()
    load_shift.wait()
    mul = rstd * gain[...].reshape(1, C_MID)
    add = (shift[...].reshape(1, C_MID) - mean * mul) * 0.5
    mul = mul * 0.5

    def activate(r, c):
        arow = 4 * b - 1 + r
        row_ok = jnp.logical_and(arow >= 0, arow < HL)
        a = []
        for f in range(4):
            ok = jnp.where(jnp.logical_and(row_ok, 2 * s - 2 + f >= 0), 1.0, 0.0)
            hv = x0s[f, r].astype(F32) * (mul[f : f + 1] * ok) + add[f : f + 1] * ok
            a.append(hv + hv * jnp.tanh(hv))
        for i, v in enumerate((a[0] - a[2], a[1] + a[2], a[2] - a[1], a[1] - a[3])):
            for dx, w in enumerate(col_shifts(v)):
                v3[i, r, :, dx * C_MID : (dx + 1) * C_MID] = w.astype(BF)
        return c

    lax.fori_loop(0, 6, activate, 0)

    def halo_copy(up):
        return pltpu.make_async_remote_copy(
            src_ref=x1s.at[:, 1 if up else RB],
            dst_ref=x1s.at[:, RB + 1 if up else 0],
            send_sem=hsend_sem.at[0 if up else 1],
            recv_sem=hrecv_sem.at[0 if up else 1],
            device_id={"seg": s, "band": b - 1 if up else b + 1},
            device_id_type=MESH,
        )

    def widen(f, r, v):
        for dx, w in enumerate(col_shifts(v)):
            x3[f, r, :, dx * C_MID : (dx + 1) * C_MID] = w.astype(BF)

    def residual(h, c):
        ra, rb = h, 3 - h

        def product(i):
            acc = None
            for dy in range(3):
                x = jnp.concatenate([v3[i, ra + dy], v3[i, rb + dy]], axis=0)
                ks = slice(dy * TAPW, (dy + 1) * TAPW)
                g = (wm[0, ks, :], gs[0, ks, :], gs[1, ks, :], wm[2, ks, :])[i]
                d = jnp.dot(x, g, preferred_element_type=F32)
                acc = d if acc is None else acc + d
            return acc

        t1, t2, t3, t4 = (product(i) for i in range(4))
        for f, y in enumerate((t1 + t2 + t3, t2 - t3 - t4)):
            for r, part in ((ra, y[:COLS]), (rb, y[COLS:])):
                x1 = (x0s[FR + f, 1 + r].astype(F32) + part).astype(BF)
                x1s[f, 1 + r] = x1
                widen(f, 1 + r, x1.astype(F32))

        @pl.when(h == 0)
        def _():
            pl.when(b > 0)(lambda: halo_copy(True).start())
            pl.when(b < BANDS - 1)(lambda: halo_copy(False).start())

        return c

    lax.fori_loop(0, 2, residual, 0)

    @pl.when(b > 0)
    def _():
        halo_copy(False).wait_recv()

    @pl.when(b < BANDS - 1)
    def _():
        halo_copy(True).wait_recv()

    for f in range(FR):
        widen(f, 0, jnp.where(b > 0, x1s[f, 0].astype(F32), 0.0))
        widen(f, RB + 1, jnp.where(b < BANDS - 1, x1s[f, RB + 1].astype(F32), 0.0))

    def upsample(f, c):
        for r2 in range(2):
            y = []
            for c2 in range(2):
                acc = None
                for rt in range(2):
                    x = x3[f, r2 + rt : r2 + rt + RB, :, c2 * C_MID : (c2 + 2) * C_MID].reshape(RB * COLS, 2 * C_MID)
                    d = lax.dot_general(
                        x, u[r2 * 2 + c2, :, rt * 2 * C_MID : (rt + 1) * 2 * C_MID],
                        (((1,), (1,)), ((), ())), preferred_element_type=F32,
                    )
                    acc = d if acc is None else acc + d
                y.append(acc)
            full = jnp.concatenate([y[0][:, :128], y[0][:, 128:] + y[1][:, :128], y[1][:, 128:]], axis=1)
            for p in range(RB):
                for l in range(3):
                    zs[l, pl.ds(2 * p + r2, COLS, stride=8), :] = full[p * COLS : (p + 1) * COLS, l * 128 : (l + 1) * 128]
        for q in range(COLS):
            for l in range(3):
                at = q * 2 * C_OUT + l * 128
                out[f, :, at : at + 128] = zs[l, q * 8 : (q + 1) * 8, :].astype(BF)
        return c

    lax.fori_loop(0, FR, upsample, 0)

    pl.when(b > 0)(lambda: halo_copy(True).wait_send())
    pl.when(b < BANDS - 1)(lambda: halo_copy(False).wait_send())
    each_latent_copy(lambda ds, tb: latent_copy(ds, tb).wait_send())
    for tb in range(BANDS):
        pl.when(b != tb)(lambda tb=tb: stat_copy(tb).wait_send())


def local(segs, latents, weight_in, weight_mid, weight_up, norm_gain, norm_shift):
    operands = (latents, weight_in, weight_mid, weight_up.T, norm_gain, norm_shift)
    return pl.pallas_call(
        functools.partial(decoder_kernel, segs),
        out_shape=pltpu.VMEM((FR, 2 * RB, 2 * COLS * C_OUT), BF),
        in_specs=[pl.BlockSpec(memory_space=pltpu.HBM)] * 6,
        out_specs=pl.BlockSpec(memory_space=pltpu.VMEM),
        scratch_shapes=[
            pltpu.VMEM((8, COLS * C_LAT), BF),
            pltpu.VMEM((C_MID,), F32),
            pltpu.VMEM((C_MID,), F32),
            pltpu.VMEM((3, 9 * C_LAT, C_MID), BF),
            pltpu.VMEM((C_OUT, 9 * C_MID), BF),
            pltpu.VMEM((COLS, 128), BF),
            pltpu.VMEM((12, COLS, 128), BF),
            pltpu.VMEM((4 * COLS, 3 * 384), BF),
            pltpu.VMEM((3, 3 * 384, 2 * C_MID), BF),
            pltpu.VMEM((4, RB + 2, COLS, C_MID), BF),
            pltpu.VMEM((3, 9 * C_MID, C_MID), BF),
            pltpu.VMEM((2, 9 * C_MID, C_MID), BF),
            pltpu.VMEM((8, C_MID), F32),
            pltpu.VMEM((BANDS, 8, C_MID), F32),
            pltpu.VMEM((4, RB + 2, COLS, TAPW), BF),
            pltpu.VMEM((FR, RB + 2, COLS, C_MID), BF),
            pltpu.VMEM((4, 256, 4 * C_MID), BF),
            pltpu.VMEM((FR, RB + 2, COLS, TAPW), BF),
            pltpu.VMEM((3, COLS * 8, 128), F32),
            pltpu.SemaphoreType.DMA((6,)),
            pltpu.SemaphoreType.DMA((12,)),
            pltpu.SemaphoreType.DMA((12,)),
            pltpu.SemaphoreType.DMA((BANDS,)),
            pltpu.SemaphoreType.DMA((BANDS,)),
            pltpu.SemaphoreType.DMA((2,)),
            pltpu.SemaphoreType.DMA((2,)),
        ],
        compiler_params=pltpu.CompilerParams(collective_id=0, has_side_effects=True, vmem_limit_bytes=58 << 20),
        name="decoder",
    )(*(pltpu.with_memory_space_constraint(x, pltpu.HBM) for x in operands))


def solution(mesh):
    return jax.shard_map(
        functools.partial(local, mesh.shape["seg"]),
        mesh=mesh,
        in_specs=(P(("seg", "band"), None), P(), P(), P(), P(), P()),
        out_specs=P("seg", "band", None),
        check_vma=False,
    )
```

```python
import functools

import jax
import jax.numpy as jnp
from jax import lax
from jax.experimental import pallas as pl
from jax.experimental.pallas import tpu as pltpu
from jax.sharding import PartitionSpec as P

C_LAT = 16
C_MID = 384
C_OUT = 192
GROUPS = 32
COLS = 160
HL = 16
FR = 2
RB = 4
BANDS = 4
CELLS = HL * COLS * (C_MID // GROUPS)
TAPW = 3 * C_MID
PAIRS = ((1, 2), (3, 4), (0, 5))
EARLY = 40
MADE = [(i, k) for i in range(4) for k in range(4) if i in (1, 2) or k in (1, 2)]
MESH = pl.DeviceIdType.MESH
BF = jnp.bfloat16
F32 = jnp.float32


def col_shifts(v):
    cols = v.shape[0]
    j = lax.broadcasted_iota(jnp.int32, v.shape, 0)
    before = jnp.where(j == 0, 0.0, pltpu.roll(v, 1, 0))
    after = jnp.where(j == cols - 1, 0.0, pltpu.roll(v, cols - 1, 0))
    return before, v, after


def columns_first(lat):
    blocks = COLS * C_LAT // 128
    x = jnp.concatenate([lat[:, k * 128 : (k + 1) * 128].astype(F32)[None] for k in range(blocks)], axis=0)
    row = lax.broadcasted_iota(jnp.int32, x.shape, 1)
    col = lax.broadcasted_iota(jnp.int32, x.shape, 2) // C_LAT
    for k in (1, 2, 4):
        r, c = (row // k) % 2, (col // k) % 2
        from_below = pltpu.roll(pltpu.roll(x, k * C_LAT, 2), 8 - k, 1)
        from_above = pltpu.roll(pltpu.roll(x, 128 - k * C_LAT, 2), k, 1)
        x = jnp.where(r == c, x, jnp.where(r < c, from_below, from_above))
    return x.reshape(COLS, 128).astype(BF)


def decoder_kernel(
    segs, lat_hbm, w_in_hbm, w_mid, w_up_hbm, gain_hbm, shift_hbm, out,
    lat, gain, shift, w_in, w_upt, z, lrecv, lst, wb, x0s, act, wm, hs, st_src, st_recv, taps, prod, ysum, rsum, x1s, u, zs,
    wsem, lsend_sem, lrecv_sem, ssend_sem, srecv_sem, hsend_sem, hrecv_sem,
):
    s = lax.axis_index("seg")
    b = lax.axis_index("band")
    half = lax.rem(b, 2)

    load_in = pltpu.make_async_copy(w_in_hbm, w_in, wsem.at[0])
    load_up = pltpu.make_async_copy(w_up_hbm, w_upt, wsem.at[1])
    load_w = pltpu.make_async_copy(w_mid, wm, wsem.at[2])
    load_lat = pltpu.make_async_copy(lat_hbm, lat, wsem.at[3])
    load_gain = pltpu.make_async_copy(gain_hbm, gain, wsem.at[4])
    load_shift = pltpu.make_async_copy(shift_hbm, shift, wsem.at[5])
    for load in (load_lat, load_in, load_up, load_w, load_gain, load_shift):
        load.start()

    barrier = pltpu.get_barrier_semaphore()

    def each_peer(fn):
        for ds in range(-2, 3):
            for tb in range(BANDS):
                ok = jnp.logical_and(s + ds >= 0, s + ds < segs)
                if ds == 0:
                    ok = jnp.logical_and(ok, b != tb)
                pl.when(ok)(functools.partial(fn, ds, tb))

    def greet(ds, tb):
        pl.semaphore_signal(barrier, inc=1, device_id={"seg": s + ds, "band": jnp.int32(tb)}, device_id_type=MESH)

    peers = -1
    for ds in range(-2, 3):
        ok = jnp.logical_and(s + ds >= 0, s + ds < segs)
        peers = peers + jnp.where(ok, BANDS, 0)

    each_peer(greet)
    load_lat.wait()
    z[...] = columns_first(lat)

    load_in.wait()
    for q, pair in enumerate(PAIRS):
        for k, r in enumerate(pair):
            for t in range(3):
                for dx in range(3):
                    for rw in range(8):
                        dy = rw - r
                        at = t * 384 + dx * 128 + rw * 16
                        if 0 <= dy < 3:
                            blk = w_in[t, (dy * 3 + dx) * 16 : (dy * 3 + dx + 1) * 16, :]
                        else:
                            blk = jnp.zeros((16, C_MID), BF)
                        wb[q, at : at + 16, k * C_MID : (k + 1) * C_MID] = blk

    pl.semaphore_wait(barrier, peers)

    def latent_copy(ds, tb):
        return pltpu.make_async_remote_copy(
            src_ref=z,
            dst_ref=lrecv.at[8 - 4 * ds + b],
            send_sem=lsend_sem.at[ds * BANDS + tb],
            recv_sem=lrecv_sem.at[8 - 4 * ds + b],
            device_id={"seg": s + ds, "band": jnp.int32(tb)},
            device_id_type=MESH,
        )

    def each_latent_copy(fn):
        for ds in range(3):
            for tb in range(BANDS):
                ok = s + ds < segs
                if tb == 0:
                    ok = jnp.logical_and(ok, half == 0)
                if tb == BANDS - 1:
                    ok = jnp.logical_and(ok, half == 1)
                if ds == 0:
                    ok = jnp.logical_and(ok, b != tb)
                pl.when(ok)(functools.partial(fn, ds, tb))

    each_latent_copy(lambda ds, tb: latent_copy(ds, tb).start())
    lrecv[8 + b] = z[...]

    load_up.wait()
    sets = (((0,), (1, 2)), ((0, 1), (2,)))
    for c2 in range(2):
        for m, (rows, sign) in enumerate((((0, 1, 2), 1.0), ((0,), -1.0), ((2,), 1.0))):
            n0 = 64 * c2
            for ct in range(2):
                acc = None
                for dy in rows:
                    for dx in sets[c2][ct]:
                        w = w_upt[:, (dy * 3 + dx) * C_MID : (dy * 3 + dx + 1) * C_MID].astype(F32)
                        acc = w if acc is None else acc + w
                u[c2 * 3 + m, n0 : n0 + C_OUT, ct * C_MID : (ct + 1) * C_MID] = (acc * sign).astype(BF)
            z0 = C_OUT if c2 == 0 else 0
            u[c2 * 3 + m, z0 : z0 + 64, :] = jnp.zeros((64, 2 * C_MID), BF)

    load_w.wait()

    def combos(g):
        outer, mid = (g[0] + g[2]) * 0.5, g[1] * 0.5
        return g[0], outer + mid, outer - mid, g[2]

    def combine(c, carry):
        at = pl.multiple_of(c * 16, 16)
        by_dy = []
        for dy in range(3):
            by_dy.append(combos([wm[t, pl.ds(dy * TAPW + at, 16), :].astype(F32) for t in range(3)]))
        for i in range(4):
            for k, h in enumerate(combos([by_dy[dy][i] for dy in range(3)])):
                if (i, k) in MADE:
                    hs[MADE.index((i, k)), pl.ds(at, 16), :] = h.astype(BF)
        return carry

    lax.fori_loop(0, EARLY, combine, 0)

    def arrived(slot):
        pltpu.make_async_remote_copy(
            src_ref=z,
            dst_ref=lrecv.at[slot],
            send_sem=lsend_sem.at[0],
            recv_sem=lrecv_sem.at[slot],
            device_id={"seg": s, "band": b},
            device_id_type=MESH,
        ).wait_recv()

    for slot in range(12):
        ok = s - 2 + slot // 4 >= 0
        if slot % 2 == 0:
            ok = jnp.logical_and(ok, b <= 2)
        else:
            ok = jnp.logical_and(ok, b >= 1)
        if slot >= 8:
            ok = jnp.logical_and(ok, b != slot - 8)
        pl.when(ok)(functools.partial(arrived, slot))

    lane = lax.broadcasted_iota(jnp.int32, (COLS, 128), 1)
    row = 4 * b - 2 + lane // 16
    in_frame = jnp.logical_and(row >= 0, row < HL)
    for g in range(6):
        both = jnp.concatenate([lrecv[2 * g].astype(F32), lrecv[2 * g + 1].astype(F32)], axis=1)
        win = pltpu.roll(both, lax.rem(32 - 64 * b + 256, 256), 1)[:, :128]
        win = jnp.where(jnp.logical_and(in_frame, 2 * s - 4 + g >= 0), win, 0.0)
        near = jnp.concatenate(col_shifts(win), axis=1).astype(BF)
        for f in range(4):
            t = g - f
            if 0 <= t < 3:
                lst[f * COLS : (f + 1) * COLS, t * 384 : (t + 1) * 384] = near

    def conv_in(q):
        return jnp.dot(lst[...], wb[q], preferred_element_type=F32).astype(BF)

    sums = [[None] * 4, [None] * 4]
    for q, pair in enumerate(PAIRS[:2]):
        x0 = conv_in(q)
        for f in range(4):
            for k, r in enumerate(pair):
                part = x0[f * COLS : (f + 1) * COLS, k * C_MID : (k + 1) * C_MID]
                x0s[f, r] = part
                wide = part.astype(F32)
                for m, v in enumerate((wide, wide * wide)):
                    tot = jnp.sum(v, axis=0, keepdims=True)
                    sums[m][f] = tot if sums[m][f] is None else sums[m][f] + tot
    st_src[...] = jnp.concatenate(sums[0] + sums[1], axis=0)

    def stat_copy(tb):
        return pltpu.make_async_remote_copy(
            src_ref=st_src,
            dst_ref=st_recv.at[b],
            send_sem=ssend_sem.at[tb],
            recv_sem=srecv_sem.at[b],
            device_id={"seg": s, "band": jnp.int32(tb)},
            device_id_type=MESH,
        )

    for tb in range(BANDS):
        pl.when(b != tb)(lambda tb=tb: stat_copy(tb).start())
    st_recv[b] = st_src[...]

    x0 = conv_in(2)
    for f in range(4):
        for k, r in enumerate(PAIRS[2]):
            x0s[f, r] = x0[f * COLS : (f + 1) * COLS, k * C_MID : (k + 1) * C_MID]

    lax.fori_loop(EARLY, TAPW // 16, combine, 0)

    def stats_in(ob):
        pltpu.make_async_remote_copy(
            src_ref=st_src,
            dst_ref=st_recv.at[ob],
            send_sem=ssend_sem.at[0],
            recv_sem=srecv_sem.at[ob],
            device_id={"seg": s, "band": b},
            device_id_type=MESH,
        ).wait_recv()

    for ob in range(BANDS):
        pl.when(b != ob)(functools.partial(stats_in, ob))

    total = (st_recv[0] + st_recv[1]) + (st_recv[2] + st_recv[3])
    per = C_MID // GROUPS
    gi = lax.broadcasted_iota(jnp.int32, (C_MID, C_MID), 0) // per
    gj = lax.broadcasted_iota(jnp.int32, (C_MID, C_MID), 1) // per
    same = jnp.where(gi == gj, 1.0, 0.0).astype(F32)
    total = jnp.dot(total, same, preferred_element_type=F32, precision=lax.Precision.HIGHEST)
    mean = total[0:4] / CELLS
    rstd = lax.rsqrt(total[4:8] / CELLS - mean * mean + 1e-6)
    load_gain.wait()
    load_shift.wait()
    mul = rstd * gain[...].reshape(1, C_MID)
    add = (shift[...].reshape(1, C_MID) - mean * mul) * 0.5
    mul = mul * 0.5

    def activate(f, r):
        arow = 4 * b - 1 + r
        ok = jnp.logical_and(jnp.logical_and(arow >= 0, arow < HL), 2 * s - 2 + f >= 0)
        ok = jnp.where(ok, 1.0, 0.0)
        hv = x0s[f, r].astype(F32) * (mul[f : f + 1] * ok) + add[f : f + 1] * ok
        act[f, r] = (hv + hv * jnp.tanh(hv)).astype(BF)

    def spread(slot, v):
        for dx, w in enumerate(col_shifts(v)):
            taps[slot, :, dx * C_MID : (dx + 1) * C_MID] = w.astype(BF)

    def inputs(i, tau):
        v = []
        for r in range(4):
            m, n, sign = ((0, 2, -1), (1, 2, 1), (2, 1, -1), (1, 3, -1))[i]
            am, an = act[m, 2 * tau + r].astype(F32), act[n, 2 * tau + r].astype(F32)
            v.append(am + an if sign > 0 else am - an)
        for k, w in enumerate((v[0] - v[2], v[1] + v[2], v[2] - v[1], v[1] - v[3])):
            spread(i * 8 + k * 2 + tau, w)

    def product(i, k):
        if (i, k) in MADE:
            g = hs[MADE.index((i, k))]
        else:
            at = 0 if k == 0 else 2 * TAPW
            g = wm[0 if i == 0 else 2, at : at + TAPW, :]
        at = i * 8 + k * 2
        to = prod.at[i % 2, k % 2]
        to[...] = jnp.dot(taps[at : at + 2].reshape(2 * COLS, TAPW), g, preferred_element_type=F32)
        return to

    def add_to(sums, k, to):
        if k == 0:
            sums[0] = to[...]
        elif k == 1:
            sums[0] += to[...]
            sums[1] = to[...]
        elif k == 2:
            sums[0] += to[...]
            sums[1] -= to[...]
        else:
            sums[1] -= to[...]

    def middle(r, c):
        activate(1, r)
        activate(2, r)
        return c

    lax.fori_loop(0, RB + 2, middle, 0)

    def first_inputs(tau, c):
        inputs(1, tau)
        return c

    lax.fori_loop(0, 2, first_inputs, 0)

    def stage(i, sums, beside):
        for k in range(4):
            add_to(sums, k, product(i, k))
            for fn in beside[k]:
                fn()

    def later(fn, *args):
        return functools.partial(fn, *args)

    def outer_work(i):
        rows = [later(activate, i, r) for r in range(RB + 2)]
        return rows[:3], rows[3:], [later(inputs, i, 0)], [later(inputs, i, 1)]

    stage(1, ysum.at[0], ([later(inputs, 2, 0)], [later(inputs, 2, 1)], [], []))
    stage(2, ysum.at[1], outer_work(0))
    for par in range(2):
        t1, t2 = ysum[0, par], ysum[1, par]
        ysum[0, par] = t1 + t2
        ysum[1, par] = t1 - t2

    def x3_slot(f, p):
        return f * 7 + p

    def d3_slot(f, p):
        return {0: 14, RB: 16}[p] + f if p in (0, RB) else f * 7 + RB + p - 1

    def halo_copy(f, up):
        return pltpu.make_async_remote_copy(
            src_ref=x1s.at[f, 1 if up else RB],
            dst_ref=x1s.at[f, RB + 1 if up else 0],
            send_sem=hsend_sem.at[f, 0 if up else 1],
            recv_sem=hrecv_sem.at[f, 0 if up else 1],
            device_id={"seg": s, "band": b - 1 if up else b + 1},
            device_id_type=MESH,
        )

    def finish(f, beside):
        stage(3 * f, rsum, beside)
        for par in range(2):
            y = ysum[f, par] + rsum[par] if f == 0 else ysum[f, par] - rsum[par]
            for tau in range(2):
                r = 1 + 2 * tau + par
                x1s[f, r] = (x0s[FR + f, r].astype(F32) + y[tau * COLS : (tau + 1) * COLS]).astype(BF)

    def send(f):
        pl.when(b > 0)(lambda: halo_copy(f, True).start())
        pl.when(b < BANDS - 1)(lambda: halo_copy(f, False).start())

    def receive(f):
        pl.when(b > 0)(lambda: halo_copy(f, False).wait_recv())
        pl.when(b < BANDS - 1)(lambda: halo_copy(f, True).wait_recv())

    def own_taps(f):
        rows = [x1s[f, 1 + p].astype(F32) for p in range(RB)]
        for p in range(RB):
            spread(x3_slot(f, p), rows[p])
            if p:
                spread(d3_slot(f, p), rows[p] - rows[p - 1])

    def edge_taps(f):
        above = jnp.where(b > 0, x1s[f, 0].astype(F32), 0.0)
        below = jnp.where(b < BANDS - 1, x1s[f, RB + 1].astype(F32), 0.0)
        spread(d3_slot(f, 0), x1s[f, 1].astype(F32) - above)
        spread(d3_slot(f, RB), below - x1s[f, RB].astype(F32))

    def phase(c2, m, slot, rows):
        x = taps[slot : slot + rows, :, c2 * C_MID : (c2 + 2) * C_MID].reshape(rows * COLS, 2 * C_MID)
        return lax.dot_general(x, u[c2 * 3 + m], (((1,), (1,)), ((), ())), preferred_element_type=F32)

    def place(f, r2, p0, y):
        full = (y[0][:, :128], y[0][:, 128:] + y[1][:, :128], y[1][:, 128:])
        for p in range(y[0].shape[0] // COLS):
            for l in range(3):
                at = pl.ds(2 * (p0 + p) + r2, COLS, stride=8)
                zs[f, l, at, :] = full[l][p * COLS : (p + 1) * COLS]

    def inner_rows(f):
        even, odd = [], []
        for c2 in range(2):
            mid = phase(c2, 0, x3_slot(f, 0), RB)
            even.append(mid[COLS:] + phase(c2, 1, d3_slot(f, 1), RB - 1))
            odd.append(mid[:-COLS] + phase(c2, 2, d3_slot(f, 1), RB - 1))
            prod[f, c2, :COLS, :256] = mid[:COLS]
            prod[f, c2, COLS:, :256] = mid[-COLS:]
        place(f, 0, 1, even)
        place(f, 1, 0, odd)

    def edge_rows():
        for e, (m, p, row) in enumerate(((1, 0, 0), (2, RB, RB - 1))):
            d = [phase(c2, m, d3_slot(0, p), FR) for c2 in range(2)]
            for f in range(FR):
                y = [prod[f, c2, e * COLS : (e + 1) * COLS, :256] + d[c2][f * COLS : (f + 1) * COLS] for c2 in range(2)]
                place(f, e, row, y)

    def pack(f):
        for q in range(COLS):
            for l in range(3):
                at = q * 2 * C_OUT + l * 128
                out[f, :, at : at + 128] = zs[f, l, q * 8 : (q + 1) * 8, :].astype(BF)

    finish(0, outer_work(3))
    send(0)
    finish(1, ([], [], [later(own_taps, 0)], []))
    send(1)
    own_taps(1)
    inner_rows(0)
    inner_rows(1)
    for f in range(FR):
        receive(f)
    for f in range(FR):
        edge_taps(f)
    edge_rows()
    for f in range(FR):
        pack(f)

    for f in range(FR):
        pl.when(b > 0)(lambda f=f: halo_copy(f, True).wait_send())
        pl.when(b < BANDS - 1)(lambda f=f: halo_copy(f, False).wait_send())
    each_latent_copy(lambda ds, tb: latent_copy(ds, tb).wait_send())
    for tb in range(BANDS):
        pl.when(b != tb)(lambda tb=tb: stat_copy(tb).wait_send())


def local(segs, latents, weight_in, weight_mid, weight_up, norm_gain, norm_shift):
    operands = (latents, weight_in, weight_mid, weight_up.T, norm_gain, norm_shift)
    return pl.pallas_call(
        functools.partial(decoder_kernel, segs),
        out_shape=pltpu.VMEM((FR, 2 * RB, 2 * COLS * C_OUT), BF),
        in_specs=[pl.BlockSpec(memory_space=pltpu.HBM)] * 6,
        out_specs=pl.BlockSpec(memory_space=pltpu.VMEM),
        scratch_shapes=[
            pltpu.VMEM((8, COLS * C_LAT), BF),
            pltpu.VMEM((C_MID,), F32),
            pltpu.VMEM((C_MID,), F32),
            pltpu.VMEM((3, 9 * C_LAT, C_MID), BF),
            pltpu.VMEM((C_OUT, 9 * C_MID), BF),
            pltpu.VMEM((COLS, 128), BF),
            pltpu.VMEM((12, COLS, 128), BF),
            pltpu.VMEM((4 * COLS, 3 * 384), BF),
            pltpu.VMEM((3, 3 * 384, 2 * C_MID), BF),
            pltpu.VMEM((4, RB + 2, COLS, C_MID), BF),
            pltpu.VMEM((4, RB + 2, COLS, C_MID), BF),
            pltpu.VMEM((3, 9 * C_MID, C_MID), BF),
            pltpu.VMEM((len(MADE), TAPW, C_MID), BF),
            pltpu.VMEM((8, C_MID), F32),
            pltpu.VMEM((BANDS, 8, C_MID), F32),
            pltpu.VMEM((32, COLS, TAPW), BF),
            pltpu.VMEM((2, 2, 2 * COLS, C_MID), F32),
            pltpu.VMEM((FR, 2, 2 * COLS, C_MID), F32),
            pltpu.VMEM((2, 2 * COLS, C_MID), F32),
            pltpu.VMEM((FR, RB + 2, COLS, C_MID), BF),
            pltpu.VMEM((6, 256, 2 * C_MID), BF),
            pltpu.VMEM((FR, 3, COLS * 8, 128), F32),
            pltpu.SemaphoreType.DMA((6,)),
            pltpu.SemaphoreType.DMA((12,)),
            pltpu.SemaphoreType.DMA((12,)),
            pltpu.SemaphoreType.DMA((BANDS,)),
            pltpu.SemaphoreType.DMA((BANDS,)),
            pltpu.SemaphoreType.DMA((FR, 2)),
            pltpu.SemaphoreType.DMA((FR, 2)),
        ],
        compiler_params=pltpu.CompilerParams(collective_id=0, has_side_effects=True, vmem_limit_bytes=60 << 20),
        name="decoder",
    )(*(pltpu.with_memory_space_constraint(x, pltpu.HBM) for x in operands))


def solution(mesh):
    return jax.shard_map(
        functools.partial(local, mesh.shape["seg"]),
        mesh=mesh,
        in_specs=(P(("seg", "band"), None), P(), P(), P(), P(), P()),
        out_specs=P("seg", "band", None),
        check_vma=False,
    )
```

```python
import functools

import jax
import jax.numpy as jnp
from jax import lax
from jax.experimental import pallas as pl
from jax.experimental.pallas import tpu as pltpu
from jax.sharding import PartitionSpec as P

C_LAT = 16
C_MID = 384
C_OUT = 192
GROUPS = 32
COLS = 160
HL = 16
FR = 2
RB = 4
BANDS = 4
CELLS = HL * COLS * (C_MID // GROUPS)
TAPW = 3 * C_MID
PAIRS = ((1, 2), (3, 4), (0, 5))
QC = COLS // 4
EARLY = 40
MADE = [(i, k) for i in range(4) for k in range(4) if i in (1, 2) or k in (1, 2)]
MESH = pl.DeviceIdType.MESH
BF = jnp.bfloat16
F32 = jnp.float32


def col_shifts(v):
    cols = v.shape[0]
    j = lax.broadcasted_iota(jnp.int32, v.shape, 0)
    before = jnp.where(j == 0, 0.0, pltpu.roll(v, 1, 0))
    after = jnp.where(j == cols - 1, 0.0, pltpu.roll(v, cols - 1, 0))
    return before, v, after


def columns_first(lat):
    blocks = COLS * C_LAT // 128
    x = jnp.concatenate([lat[:, k * 128 : (k + 1) * 128].astype(F32)[None] for k in range(blocks)], axis=0)
    row = lax.broadcasted_iota(jnp.int32, x.shape, 1)
    col = lax.broadcasted_iota(jnp.int32, x.shape, 2) // C_LAT
    for k in (1, 2, 4):
        r, c = (row // k) % 2, (col // k) % 2
        from_below = pltpu.roll(pltpu.roll(x, k * C_LAT, 2), 8 - k, 1)
        from_above = pltpu.roll(pltpu.roll(x, 128 - k * C_LAT, 2), k, 1)
        x = jnp.where(r == c, x, jnp.where(r < c, from_below, from_above))
    x = x.reshape(COLS, 128)
    return [x[q * QC : (q + 1) * QC] for q in range(4)]


def swap_quarters(x):
    group = lax.broadcasted_iota(jnp.int32, (QC, 128), 1) // 32
    x = list(x)
    for m in (1, 2):
        bit = (group // m) % 2
        for q in range(4):
            if not q & m:
                lo, hi = x[q], x[q | m]
                x[q] = jnp.where(bit == 0, lo, pltpu.roll(hi, m * 32, 1))
                x[q | m] = jnp.where(bit == 1, hi, pltpu.roll(lo, 128 - m * 32, 1))
    return x


def decoder_kernel(
    segs, lat_hbm, w_in_hbm, w_mid, w_up_hbm, gain_hbm, shift_hbm, out,
    lat, gain, shift, w_in, w_upt, z, lrecv, lst, wb, x0s, act, wm, hs, st_src, st_recv, taps, prod, ysum, rsum, x1s, u, zs,
    wsem, lsend_sem, lrecv_sem, ssend_sem, srecv_sem, hsend_sem, hrecv_sem,
):
    s = lax.axis_index("seg")
    b = lax.axis_index("band")
    half = lax.rem(b, 2)

    load_in = pltpu.make_async_copy(w_in_hbm, w_in, wsem.at[0])
    load_up = pltpu.make_async_copy(w_up_hbm, w_upt, wsem.at[1])
    load_w = pltpu.make_async_copy(w_mid, wm, wsem.at[2])
    load_lat = pltpu.make_async_copy(lat_hbm, lat, wsem.at[3])
    load_gain = pltpu.make_async_copy(gain_hbm, gain, wsem.at[4])
    load_shift = pltpu.make_async_copy(shift_hbm, shift, wsem.at[5])
    for load in (load_lat, load_in, load_up, load_w, load_gain, load_shift):
        load.start()

    barrier = pltpu.get_barrier_semaphore()

    def each_peer(fn):
        for ds in range(-2, 3):
            for tb in range(BANDS):
                ok = jnp.logical_and(s + ds >= 0, s + ds < segs)
                if ds == 0:
                    ok = jnp.logical_and(ok, b != tb)
                pl.when(ok)(functools.partial(fn, ds, tb))

    def greet(ds, tb):
        pl.semaphore_signal(barrier, inc=1, device_id={"seg": s + ds, "band": jnp.int32(tb)}, device_id_type=MESH)

    peers = -1
    for ds in range(-2, 3):
        ok = jnp.logical_and(s + ds >= 0, s + ds < segs)
        peers = peers + jnp.where(ok, BANDS, 0)

    each_peer(greet)
    load_lat.wait()
    for k, v in enumerate(swap_quarters(columns_first(lat))):
        z[k] = v.astype(BF)

    load_in.wait()
    for q, pair in enumerate(PAIRS):
        for k, r in enumerate(pair):
            for t in range(3):
                for dx in range(3):
                    for rw in range(8):
                        dy = rw - r
                        at = t * 384 + dx * 128 + rw * 16
                        if 0 <= dy < 3:
                            blk = w_in[t, (dy * 3 + dx) * 16 : (dy * 3 + dx + 1) * 16, :]
                        else:
                            blk = jnp.zeros((16, C_MID), BF)
                        wb[q, at : at + 16, k * C_MID : (k + 1) * C_MID] = blk

    pl.semaphore_wait(barrier, peers)

    needs = {(0, 0): (0, 1, 3), (0, 1): (1, 0, 3), (0, 2): (3, 0, 1), (1, 1): (0, 3, 1), (1, 2): (0, 1, 3), (1, 3): (1, 0, 3)}

    def latent_copy(ds, tb, h):
        src, dst, n = needs[h, tb]
        return pltpu.make_async_remote_copy(
            src_ref=z.at[src : src + n],
            dst_ref=lrecv.at[4 - 2 * ds + b // 2, dst : dst + n],
            send_sem=lsend_sem.at[ds * BANDS + tb],
            recv_sem=lrecv_sem.at[8 - 4 * ds + b],
            device_id={"seg": s + ds, "band": jnp.int32(tb)},
            device_id_type=MESH,
        )

    def each_latent_copy(fn):
        for ds in range(3):
            for h, tb in needs:
                ok = jnp.logical_and(s + ds < segs, half == h)
                if ds == 0:
                    ok = jnp.logical_and(ok, b != tb)
                pl.when(ok)(functools.partial(fn, ds, tb, h))

    each_latent_copy(lambda ds, tb, h: latent_copy(ds, tb, h).start())

    def keep(tb):
        src, dst, n = needs[tb % 2, tb]
        lrecv[4 + tb // 2, dst : dst + n] = z[src : src + n]

    for tb in range(BANDS):
        pl.when(b == tb)(functools.partial(keep, tb))

    load_up.wait()
    sets = (((0,), (1, 2)), ((0, 1), (2,)))
    for c2 in range(2):
        for m, (rows, sign) in enumerate((((0, 1, 2), 1.0), ((0,), -1.0), ((2,), 1.0))):
            n0 = 64 * c2
            for ct in range(2):
                acc = None
                for dy in rows:
                    for dx in sets[c2][ct]:
                        w = w_upt[:, (dy * 3 + dx) * C_MID : (dy * 3 + dx + 1) * C_MID].astype(F32)
                        acc = w if acc is None else acc + w
                u[c2 * 3 + m, n0 : n0 + C_OUT, ct * C_MID : (ct + 1) * C_MID] = (acc * sign).astype(BF)
            z0 = C_OUT if c2 == 0 else 0
            u[c2 * 3 + m, z0 : z0 + 64, :] = jnp.zeros((64, 2 * C_MID), BF)

    load_w.wait()

    def combos(g):
        outer, mid = (g[0] + g[2]) * 0.5, g[1] * 0.5
        return g[0], outer + mid, outer - mid, g[2]

    def combine(c, carry):
        at = pl.multiple_of(c * 16, 16)
        by_dy = []
        for dy in range(3):
            by_dy.append(combos([wm[t, pl.ds(dy * TAPW + at, 16), :].astype(F32) for t in range(3)]))
        for i in range(4):
            for k, h in enumerate(combos([by_dy[dy][i] for dy in range(3)])):
                if (i, k) in MADE:
                    hs[MADE.index((i, k)), pl.ds(at, 16), :] = h.astype(BF)
        return carry

    lax.fori_loop(0, EARLY, combine, 0)

    def arrived(g, h, tb):
        src, dst, n = needs[h, tb]
        pltpu.make_async_remote_copy(
            src_ref=z.at[src : src + n],
            dst_ref=lrecv.at[g, dst : dst + n],
            send_sem=lsend_sem.at[0],
            recv_sem=lrecv_sem.at[2 * g + h],
            device_id={"seg": s, "band": b},
            device_id_type=MESH,
        ).wait_recv()

    for g in range(6):
        for h, tb in needs:
            ok = jnp.logical_and(s - 2 + g // 2 >= 0, b == tb)
            if (g - 4) * 2 + h != tb:
                pl.when(ok)(functools.partial(arrived, g, h, tb))

    lane = lax.broadcasted_iota(jnp.int32, (COLS, 128), 1)
    row = 4 * b - 2 + lane // 16
    in_frame = jnp.logical_and(row >= 0, row < HL)
    for g in range(6):
        win = jnp.concatenate(swap_quarters([lrecv[g, k].astype(F32) for k in range(4)]), axis=0)
        win = jnp.where(jnp.logical_and(in_frame, 2 * s - 4 + g >= 0), win, 0.0)
        near = jnp.concatenate(col_shifts(win), axis=1).astype(BF)
        for f in range(4):
            t = g - f
            if 0 <= t < 3:
                lst[f * COLS : (f + 1) * COLS, t * 384 : (t + 1) * 384] = near

    def conv_in(q):
        return jnp.dot(lst[...], wb[q], preferred_element_type=F32).astype(BF)

    sums = [[None] * 4, [None] * 4]
    for q, pair in enumerate(PAIRS[:2]):
        x0 = conv_in(q)
        for f in range(4):
            for k, r in enumerate(pair):
                part = x0[f * COLS : (f + 1) * COLS, k * C_MID : (k + 1) * C_MID]
                x0s[f, r] = part
                wide = part.astype(F32)
                for m, v in enumerate((wide, wide * wide)):
                    tot = jnp.sum(v, axis=0, keepdims=True)
                    sums[m][f] = tot if sums[m][f] is None else sums[m][f] + tot
    st_src[...] = jnp.concatenate(sums[0] + sums[1], axis=0)

    def stat_copy(tb):
        return pltpu.make_async_remote_copy(
            src_ref=st_src,
            dst_ref=st_recv.at[b],
            send_sem=ssend_sem.at[tb],
            recv_sem=srecv_sem.at[b],
            device_id={"seg": s, "band": jnp.int32(tb)},
            device_id_type=MESH,
        )

    for tb in range(BANDS):
        pl.when(b != tb)(lambda tb=tb: stat_copy(tb).start())
    st_recv[b] = st_src[...]

    x0 = conv_in(2)
    for f in range(4):
        for k, r in enumerate(PAIRS[2]):
            x0s[f, r] = x0[f * COLS : (f + 1) * COLS, k * C_MID : (k + 1) * C_MID]

    lax.fori_loop(EARLY, TAPW // 16, combine, 0)

    def stats_in(ob):
        pltpu.make_async_remote_copy(
            src_ref=st_src,
            dst_ref=st_recv.at[ob],
            send_sem=ssend_sem.at[0],
            recv_sem=srecv_sem.at[ob],
            device_id={"seg": s, "band": b},
            device_id_type=MESH,
        ).wait_recv()

    for ob in range(BANDS):
        pl.when(b != ob)(functools.partial(stats_in, ob))

    total = (st_recv[0] + st_recv[1]) + (st_recv[2] + st_recv[3])
    per = C_MID // GROUPS
    gi = lax.broadcasted_iota(jnp.int32, (C_MID, C_MID), 0) // per
    gj = lax.broadcasted_iota(jnp.int32, (C_MID, C_MID), 1) // per
    same = jnp.where(gi == gj, 1.0, 0.0).astype(F32)
    total = jnp.dot(total, same, preferred_element_type=F32, precision=lax.Precision.HIGHEST)
    mean = total[0:4] / CELLS
    rstd = lax.rsqrt(total[4:8] / CELLS - mean * mean + 1e-6)
    load_gain.wait()
    load_shift.wait()
    mul = rstd * gain[...].reshape(1, C_MID)
    add = (shift[...].reshape(1, C_MID) - mean * mul) * 0.5
    mul = mul * 0.5

    def activate(f, r):
        arow = 4 * b - 1 + r
        ok = jnp.logical_and(jnp.logical_and(arow >= 0, arow < HL), 2 * s - 2 + f >= 0)
        ok = jnp.where(ok, 1.0, 0.0)
        hv = x0s[f, r].astype(F32) * (mul[f : f + 1] * ok) + add[f : f + 1] * ok
        act[f, r] = (hv + hv * jnp.tanh(hv)).astype(BF)

    def spread(slot, v):
        for dx, w in enumerate(col_shifts(v)):
            taps[slot, :, dx * C_MID : (dx + 1) * C_MID] = w.astype(BF)

    def inputs(i, tau):
        v = []
        for r in range(4):
            m, n, sign = ((0, 2, -1), (1, 2, 1), (2, 1, -1), (1, 3, -1))[i]
            am, an = act[m, 2 * tau + r].astype(F32), act[n, 2 * tau + r].astype(F32)
            v.append(am + an if sign > 0 else am - an)
        for k, w in enumerate((v[0] - v[2], v[1] + v[2], v[2] - v[1], v[1] - v[3])):
            spread(i * 8 + k * 2 + tau, w)

    def product(i, k):
        if (i, k) in MADE:
            g = hs[MADE.index((i, k))]
        else:
            at = 0 if k == 0 else 2 * TAPW
            g = wm[0 if i == 0 else 2, at : at + TAPW, :]
        at = i * 8 + k * 2
        to = prod.at[i % 2, k % 2]
        to[...] = jnp.dot(taps[at : at + 2].reshape(2 * COLS, TAPW), g, preferred_element_type=F32)
        return to

    def add_to(sums, k, to):
        if k == 0:
            sums[0] = to[...]
        elif k == 1:
            sums[0] += to[...]
            sums[1] = to[...]
        elif k == 2:
            sums[0] += to[...]
            sums[1] -= to[...]
        else:
            sums[1] -= to[...]

    def middle(r, c):
        activate(1, r)
        activate(2, r)
        return c

    lax.fori_loop(0, RB + 2, middle, 0)

    def first_inputs(tau, c):
        inputs(1, tau)
        return c

    lax.fori_loop(0, 2, first_inputs, 0)

    def stage(i, sums, beside):
        for k in range(4):
            add_to(sums, k, product(i, k))
            for fn in beside[k]:
                fn()

    def later(fn, *args):
        return functools.partial(fn, *args)

    def outer_work(i):
        rows = [later(activate, i, r) for r in range(RB + 2)]
        return rows[:3], rows[3:], [later(inputs, i, 0)], [later(inputs, i, 1)]

    stage(1, ysum.at[0], ([later(inputs, 2, 0)], [later(inputs, 2, 1)], [], []))
    stage(2, ysum.at[1], outer_work(0))
    for par in range(2):
        t1, t2 = ysum[0, par], ysum[1, par]
        ysum[0, par] = t1 + t2
        ysum[1, par] = t1 - t2

    def x3_slot(f, p):
        return f * 7 + p

    def d3_slot(f, p):
        return {0: 14, RB: 16}[p] + f if p in (0, RB) else f * 7 + RB + p - 1

    def halo_copy(f, up):
        return pltpu.make_async_remote_copy(
            src_ref=x1s.at[f, 1 if up else RB],
            dst_ref=x1s.at[f, RB + 1 if up else 0],
            send_sem=hsend_sem.at[f, 0 if up else 1],
            recv_sem=hrecv_sem.at[f, 0 if up else 1],
            device_id={"seg": s, "band": b - 1 if up else b + 1},
            device_id_type=MESH,
        )

    def finish(f, beside):
        stage(3 * f, rsum, beside)
        for par in range(2):
            y = ysum[f, par] + rsum[par] if f == 0 else ysum[f, par] - rsum[par]
            for tau in range(2):
                r = 1 + 2 * tau + par
                x1s[f, r] = (x0s[FR + f, r].astype(F32) + y[tau * COLS : (tau + 1) * COLS]).astype(BF)

    def send(f):
        pl.when(b > 0)(lambda: halo_copy(f, True).start())
        pl.when(b < BANDS - 1)(lambda: halo_copy(f, False).start())

    def receive(f):
        pl.when(b > 0)(lambda: halo_copy(f, False).wait_recv())
        pl.when(b < BANDS - 1)(lambda: halo_copy(f, True).wait_recv())

    def own_taps(f):
        rows = [x1s[f, 1 + p].astype(F32) for p in range(RB)]
        for p in range(RB):
            spread(x3_slot(f, p), rows[p])
            if p:
                spread(d3_slot(f, p), rows[p] - rows[p - 1])

    def edge_taps(f):
        above = jnp.where(b > 0, x1s[f, 0].astype(F32), 0.0)
        below = jnp.where(b < BANDS - 1, x1s[f, RB + 1].astype(F32), 0.0)
        spread(d3_slot(f, 0), x1s[f, 1].astype(F32) - above)
        spread(d3_slot(f, RB), below - x1s[f, RB].astype(F32))

    def phase(c2, m, slot, rows):
        x = taps[slot : slot + rows, :, c2 * C_MID : (c2 + 2) * C_MID].reshape(rows * COLS, 2 * C_MID)
        return lax.dot_general(x, u[c2 * 3 + m], (((1,), (1,)), ((), ())), preferred_element_type=F32)

    def place(f, r2, p0, y):
        full = (y[0][:, :128], y[0][:, 128:] + y[1][:, :128], y[1][:, 128:])
        for p in range(y[0].shape[0] // COLS):
            for l in range(3):
                at = pl.ds(2 * (p0 + p) + r2, COLS, stride=8)
                zs[f, l, at, :] = full[l][p * COLS : (p + 1) * COLS]

    def inner_rows(f):
        even, odd = [], []
        for c2 in range(2):
            mid = phase(c2, 0, x3_slot(f, 0), RB)
            even.append(mid[COLS:] + phase(c2, 1, d3_slot(f, 1), RB - 1))
            odd.append(mid[:-COLS] + phase(c2, 2, d3_slot(f, 1), RB - 1))
            prod[f, c2, :COLS, :256] = mid[:COLS]
            prod[f, c2, COLS:, :256] = mid[-COLS:]
        place(f, 0, 1, even)
        place(f, 1, 0, odd)

    def edge_rows():
        for e, (m, p, row) in enumerate(((1, 0, 0), (2, RB, RB - 1))):
            d = [phase(c2, m, d3_slot(0, p), FR) for c2 in range(2)]
            for f in range(FR):
                y = [prod[f, c2, e * COLS : (e + 1) * COLS, :256] + d[c2][f * COLS : (f + 1) * COLS] for c2 in range(2)]
                place(f, e, row, y)

    def pack(f):
        for q in range(COLS):
            for l in range(3):
                at = q * 2 * C_OUT + l * 128
                out[f, :, at : at + 128] = zs[f, l, q * 8 : (q + 1) * 8, :].astype(BF)

    finish(0, outer_work(3))
    send(0)
    finish(1, ([], [], [later(own_taps, 0)], []))
    send(1)
    own_taps(1)
    inner_rows(0)
    inner_rows(1)
    for f in range(FR):
        receive(f)
    for f in range(FR):
        edge_taps(f)
    edge_rows()
    for f in range(FR):
        pack(f)

    for f in range(FR):
        pl.when(b > 0)(lambda f=f: halo_copy(f, True).wait_send())
        pl.when(b < BANDS - 1)(lambda f=f: halo_copy(f, False).wait_send())
    each_latent_copy(lambda ds, tb, h: latent_copy(ds, tb, h).wait_send())
    for tb in range(BANDS):
        pl.when(b != tb)(lambda tb=tb: stat_copy(tb).wait_send())


def local(segs, latents, weight_in, weight_mid, weight_up, norm_gain, norm_shift):
    operands = (latents, weight_in, weight_mid, weight_up.T, norm_gain, norm_shift)
    return pl.pallas_call(
        functools.partial(decoder_kernel, segs),
        out_shape=pltpu.VMEM((FR, 2 * RB, 2 * COLS * C_OUT), BF),
        in_specs=[pl.BlockSpec(memory_space=pltpu.HBM)] * 6,
        out_specs=pl.BlockSpec(memory_space=pltpu.VMEM),
        scratch_shapes=[
            pltpu.VMEM((8, COLS * C_LAT), BF),
            pltpu.VMEM((C_MID,), F32),
            pltpu.VMEM((C_MID,), F32),
            pltpu.VMEM((3, 9 * C_LAT, C_MID), BF),
            pltpu.VMEM((C_OUT, 9 * C_MID), BF),
            pltpu.VMEM((4, QC, 128), BF),
            pltpu.VMEM((6, 4, QC, 128), BF),
            pltpu.VMEM((4 * COLS, 3 * 384), BF),
            pltpu.VMEM((3, 3 * 384, 2 * C_MID), BF),
            pltpu.VMEM((4, RB + 2, COLS, C_MID), BF),
            pltpu.VMEM((4, RB + 2, COLS, C_MID), BF),
            pltpu.VMEM((3, 9 * C_MID, C_MID), BF),
            pltpu.VMEM((len(MADE), TAPW, C_MID), BF),
            pltpu.VMEM((8, C_MID), F32),
            pltpu.VMEM((BANDS, 8, C_MID), F32),
            pltpu.VMEM((32, COLS, TAPW), BF),
            pltpu.VMEM((2, 2, 2 * COLS, C_MID), F32),
            pltpu.VMEM((FR, 2, 2 * COLS, C_MID), F32),
            pltpu.VMEM((2, 2 * COLS, C_MID), F32),
            pltpu.VMEM((FR, RB + 2, COLS, C_MID), BF),
            pltpu.VMEM((6, 256, 2 * C_MID), BF),
            pltpu.VMEM((FR, 3, COLS * 8, 128), F32),
            pltpu.SemaphoreType.DMA((6,)),
            pltpu.SemaphoreType.DMA((12,)),
            pltpu.SemaphoreType.DMA((12,)),
            pltpu.SemaphoreType.DMA((BANDS,)),
            pltpu.SemaphoreType.DMA((BANDS,)),
            pltpu.SemaphoreType.DMA((FR, 2)),
            pltpu.SemaphoreType.DMA((FR, 2)),
        ],
        compiler_params=pltpu.CompilerParams(collective_id=0, has_side_effects=True, vmem_limit_bytes=60 << 20),
        name="decoder",
    )(*(pltpu.with_memory_space_constraint(x, pltpu.HBM) for x in operands))


def solution(mesh):
    return jax.shard_map(
        functools.partial(local, mesh.shape["seg"]),
        mesh=mesh,
        in_specs=(P(("seg", "band"), None), P(), P(), P(), P(), P()),
        out_specs=P("seg", "band", None),
        check_vma=False,
    )
```

```python
import functools

import jax
import jax.numpy as jnp
from jax import lax
from jax.experimental import pallas as pl
from jax.experimental.pallas import tpu as pltpu
from jax.sharding import PartitionSpec as P

C_LAT = 16
C_MID = 384
C_OUT = 192
GROUPS = 32
COLS = 160
HL = 16
FR = 2
RB = 4
BANDS = 4
CELLS = HL * COLS * (C_MID // GROUPS)
TAPW = 3 * C_MID
PAIRS = ((1, 2), (3, 4), (0, 5))
QC = COLS // 4
EARLY = 40
MADE = [(i, k) for i in range(4) for k in range(4) if i in (1, 2) or k in (1, 2)]
MESH = pl.DeviceIdType.MESH
BF = jnp.bfloat16
F32 = jnp.float32


def col_shifts(v):
    cols = v.shape[0]
    j = lax.broadcasted_iota(jnp.int32, v.shape, 0)
    before = jnp.where(j == 0, 0.0, pltpu.roll(v, 1, 0))
    after = jnp.where(j == cols - 1, 0.0, pltpu.roll(v, cols - 1, 0))
    return before, v, after


def columns_first(lat):
    blocks = COLS * C_LAT // 128
    x = jnp.concatenate([lat[:, k * 128 : (k + 1) * 128].astype(F32)[None] for k in range(blocks)], axis=0)
    row = lax.broadcasted_iota(jnp.int32, x.shape, 1)
    col = lax.broadcasted_iota(jnp.int32, x.shape, 2) // C_LAT
    for k in (1, 2, 4):
        r, c = (row // k) % 2, (col // k) % 2
        from_below = pltpu.roll(pltpu.roll(x, k * C_LAT, 2), 8 - k, 1)
        from_above = pltpu.roll(pltpu.roll(x, 128 - k * C_LAT, 2), k, 1)
        x = jnp.where(r == c, x, jnp.where(r < c, from_below, from_above))
    x = x.reshape(COLS, 128)
    return [x[q * QC : (q + 1) * QC] for q in range(4)]


def swap_quarters(x):
    group = lax.broadcasted_iota(jnp.int32, (QC, 128), 1) // 32
    x = list(x)
    for m in (1, 2):
        bit = (group // m) % 2
        for q in range(4):
            if not q & m:
                lo, hi = x[q], x[q | m]
                x[q] = jnp.where(bit == 0, lo, pltpu.roll(hi, m * 32, 1))
                x[q | m] = jnp.where(bit == 1, hi, pltpu.roll(lo, 128 - m * 32, 1))
    return x


def decoder_kernel(
    segs, lat_hbm, w_in_hbm, w_mid, w_up_hbm, gain_hbm, shift_hbm, out,
    lat, gain, shift, w_in, w_upt, z, lrecv, lst, wb, x0s, act, wm, hs, st_src, st_recv, taps, prod, ysum, rsum, x1s, u, zs,
    wsem, lsend_sem, lrecv_sem, ssend_sem, srecv_sem, hsend_sem, hrecv_sem,
):
    s = lax.axis_index("seg")
    b = lax.axis_index("band")
    half = lax.rem(b, 2)

    load_in = pltpu.make_async_copy(w_in_hbm, w_in, wsem.at[0])
    load_up = pltpu.make_async_copy(w_up_hbm, w_upt, wsem.at[1])
    load_w = pltpu.make_async_copy(w_mid, wm, wsem.at[2])
    load_lat = pltpu.make_async_copy(lat_hbm, lat, wsem.at[3])
    load_gain = pltpu.make_async_copy(gain_hbm, gain, wsem.at[4])
    load_shift = pltpu.make_async_copy(shift_hbm, shift, wsem.at[5])
    for load in (load_lat, load_in, load_up, load_w, load_gain, load_shift):
        load.start()

    barrier = pltpu.get_barrier_semaphore()

    def each_peer(fn):
        for ds in range(-2, 3):
            for tb in range(BANDS):
                ok = jnp.logical_and(s + ds >= 0, s + ds < segs)
                if ds == 0:
                    ok = jnp.logical_and(ok, b != tb)
                pl.when(ok)(functools.partial(fn, ds, tb))

    def greet(ds, tb):
        pl.semaphore_signal(barrier, inc=1, device_id={"seg": s + ds, "band": jnp.int32(tb)}, device_id_type=MESH)

    peers = -1
    for ds in range(-2, 3):
        ok = jnp.logical_and(s + ds >= 0, s + ds < segs)
        peers = peers + jnp.where(ok, BANDS, 0)

    each_peer(greet)
    load_lat.wait()
    for k, v in enumerate(swap_quarters(columns_first(lat))):
        z[k] = v.astype(BF)

    load_in.wait()
    for q, pair in enumerate(PAIRS):
        for k, r in enumerate(pair):
            for t in range(3):
                for dx in range(3):
                    for rw in range(8):
                        dy = rw - r
                        at = t * 384 + dx * 128 + rw * 16
                        if 0 <= dy < 3:
                            blk = w_in[t, (dy * 3 + dx) * 16 : (dy * 3 + dx + 1) * 16, :]
                        else:
                            blk = jnp.zeros((16, C_MID), BF)
                        wb[q, at : at + 16, k * C_MID : (k + 1) * C_MID] = blk

    pl.semaphore_wait(barrier, peers)

    needs = {(0, 0): (0, 1, 3), (0, 1): (1, 0, 3), (0, 2): (3, 0, 1), (1, 1): (0, 3, 1), (1, 2): (0, 1, 3), (1, 3): (1, 0, 3)}

    def latent_copy(ds, tb, h):
        src, dst, n = needs[h, tb]
        return pltpu.make_async_remote_copy(
            src_ref=z.at[src : src + n],
            dst_ref=lrecv.at[4 - 2 * ds + b // 2, dst : dst + n],
            send_sem=lsend_sem.at[ds * BANDS + tb],
            recv_sem=lrecv_sem.at[8 - 4 * ds + b],
            device_id={"seg": s + ds, "band": jnp.int32(tb)},
            device_id_type=MESH,
        )

    def each_latent_copy(fn):
        for ds in (2, 1, 0):
            for h, tb in needs:
                ok = jnp.logical_and(s + ds < segs, half == h)
                if ds == 0:
                    ok = jnp.logical_and(ok, b != tb)
                pl.when(ok)(functools.partial(fn, ds, tb, h))

    each_latent_copy(lambda ds, tb, h: latent_copy(ds, tb, h).start())

    def keep(tb):
        src, dst, n = needs[tb % 2, tb]
        lrecv[4 + tb // 2, dst : dst + n] = z[src : src + n]

    for tb in range(BANDS):
        pl.when(b == tb)(functools.partial(keep, tb))

    load_up.wait()
    sets = (((0,), (1, 2)), ((0, 1), (2,)))
    for c2 in range(2):
        for m, (rows, sign) in enumerate((((0, 1, 2), 1.0), ((0,), -1.0), ((2,), 1.0))):
            n0 = 64 * c2
            for ct in range(2):
                acc = None
                for dy in rows:
                    for dx in sets[c2][ct]:
                        w = w_upt[:, (dy * 3 + dx) * C_MID : (dy * 3 + dx + 1) * C_MID].astype(F32)
                        acc = w if acc is None else acc + w
                u[c2 * 3 + m, n0 : n0 + C_OUT, ct * C_MID : (ct + 1) * C_MID] = (acc * sign).astype(BF)
            z0 = C_OUT if c2 == 0 else 0
            u[c2 * 3 + m, z0 : z0 + 64, :] = jnp.zeros((64, 2 * C_MID), BF)

    load_w.wait()

    def combos(g):
        outer, mid = (g[0] + g[2]) * 0.5, g[1] * 0.5
        return g[0], outer + mid, outer - mid, g[2]

    def combine(c, carry):
        at = pl.multiple_of(c * 16, 16)
        by_dy = []
        for dy in range(3):
            by_dy.append(combos([wm[t, pl.ds(dy * TAPW + at, 16), :].astype(F32) for t in range(3)]))
        for i in range(4):
            for k, h in enumerate(combos([by_dy[dy][i] for dy in range(3)])):
                if (i, k) in MADE:
                    hs[MADE.index((i, k)), pl.ds(at, 16), :] = h.astype(BF)
        return carry

    lax.fori_loop(0, EARLY, combine, 0)

    def arrived(g, h, tb):
        src, dst, n = needs[h, tb]
        pltpu.make_async_remote_copy(
            src_ref=z.at[src : src + n],
            dst_ref=lrecv.at[g, dst : dst + n],
            send_sem=lsend_sem.at[0],
            recv_sem=lrecv_sem.at[2 * g + h],
            device_id={"seg": s, "band": b},
            device_id_type=MESH,
        ).wait_recv()

    for g in range(6):
        for h, tb in needs:
            ok = jnp.logical_and(s - 2 + g // 2 >= 0, b == tb)
            if (g - 4) * 2 + h != tb:
                pl.when(ok)(functools.partial(arrived, g, h, tb))

    lane = lax.broadcasted_iota(jnp.int32, (COLS, 128), 1)
    row = 4 * b - 2 + lane // 16
    in_frame = jnp.logical_and(row >= 0, row < HL)
    for g in range(6):
        win = jnp.concatenate(swap_quarters([lrecv[g, k].astype(F32) for k in range(4)]), axis=0)
        win = jnp.where(jnp.logical_and(in_frame, 2 * s - 4 + g >= 0), win, 0.0)
        near = jnp.concatenate(col_shifts(win), axis=1).astype(BF)
        for f in range(4):
            t = g - f
            if 0 <= t < 3:
                lst[f * COLS : (f + 1) * COLS, t * 384 : (t + 1) * 384] = near

    def conv_in(q):
        return jnp.dot(lst[...], wb[q], preferred_element_type=F32).astype(BF)

    sums = [[None] * 4, [None] * 4]
    for q, pair in enumerate(PAIRS[:2]):
        x0 = conv_in(q)
        for f in range(4):
            for k, r in enumerate(pair):
                part = x0[f * COLS : (f + 1) * COLS, k * C_MID : (k + 1) * C_MID]
                x0s[f, r] = part
                wide = part.astype(F32)
                for m, v in enumerate((wide, wide * wide)):
                    tot = jnp.sum(v, axis=0, keepdims=True)
                    sums[m][f] = tot if sums[m][f] is None else sums[m][f] + tot
    st_src[...] = jnp.concatenate(sums[0] + sums[1], axis=0)

    def stat_copy(tb):
        return pltpu.make_async_remote_copy(
            src_ref=st_src,
            dst_ref=st_recv.at[b],
            send_sem=ssend_sem.at[tb],
            recv_sem=srecv_sem.at[b],
            device_id={"seg": s, "band": jnp.int32(tb)},
            device_id_type=MESH,
        )

    for tb in range(BANDS):
        pl.when(b != tb)(lambda tb=tb: stat_copy(tb).start())
    st_recv[b] = st_src[...]

    x0 = conv_in(2)
    for f in range(4):
        for k, r in enumerate(PAIRS[2]):
            x0s[f, r] = x0[f * COLS : (f + 1) * COLS, k * C_MID : (k + 1) * C_MID]

    lax.fori_loop(EARLY, TAPW // 16, combine, 0)

    def stats_in(ob):
        pltpu.make_async_remote_copy(
            src_ref=st_src,
            dst_ref=st_recv.at[ob],
            send_sem=ssend_sem.at[0],
            recv_sem=srecv_sem.at[ob],
            device_id={"seg": s, "band": b},
            device_id_type=MESH,
        ).wait_recv()

    for ob in range(BANDS):
        pl.when(b != ob)(functools.partial(stats_in, ob))

    total = (st_recv[0] + st_recv[1]) + (st_recv[2] + st_recv[3])
    per = C_MID // GROUPS
    gi = lax.broadcasted_iota(jnp.int32, (C_MID, C_MID), 0) // per
    gj = lax.broadcasted_iota(jnp.int32, (C_MID, C_MID), 1) // per
    same = jnp.where(gi == gj, 1.0, 0.0).astype(F32)
    total = jnp.dot(total, same, preferred_element_type=F32, precision=lax.Precision.HIGHEST)
    mean = total[0:4] / CELLS
    rstd = lax.rsqrt(total[4:8] / CELLS - mean * mean + 1e-6)
    load_gain.wait()
    load_shift.wait()
    mul = rstd * gain[...].reshape(1, C_MID)
    add = (shift[...].reshape(1, C_MID) - mean * mul) * 0.5
    mul = mul * 0.5

    def activate(f, r):
        arow = 4 * b - 1 + r
        ok = jnp.logical_and(jnp.logical_and(arow >= 0, arow < HL), 2 * s - 2 + f >= 0)
        ok = jnp.where(ok, 1.0, 0.0)
        hv = x0s[f, r].astype(F32) * (mul[f : f + 1] * ok) + add[f : f + 1] * ok
        act[f, r] = (hv + hv * jnp.tanh(hv)).astype(BF)

    def spread(slot, v):
        for dx, w in enumerate(col_shifts(v)):
            taps[slot, :, dx * C_MID : (dx + 1) * C_MID] = w.astype(BF)

    def inputs(i, k):
        m, n, sign = ((0, 2, -1), (1, 2, 1), (2, 1, -1), (1, 3, -1))[i]
        p, q, plus = ((0, 2, -1), (1, 2, 1), (2, 1, -1), (1, 3, -1))[k]
        for tau in range(2):
            v = []
            for r in (2 * tau + p, 2 * tau + q):
                am, an = act[m, r].astype(F32), act[n, r].astype(F32)
                v.append(am + an if sign > 0 else am - an)
            spread(i * 8 + k * 2 + tau, v[0] + v[1] if plus > 0 else v[0] - v[1])

    def product(i, k):
        if (i, k) in MADE:
            g = hs[MADE.index((i, k))]
        else:
            at = 0 if k == 0 else 2 * TAPW
            g = wm[0 if i == 0 else 2, at : at + TAPW, :]
        at = i * 8 + k * 2
        to = prod.at[i % 2, k % 2]
        to[...] = jnp.dot(taps[at : at + 2].reshape(2 * COLS, TAPW), g, preferred_element_type=F32)
        return to

    def add_to(sums, k, to):
        if k == 0:
            sums[0] = to[...]
        elif k == 1:
            sums[0] += to[...]
            sums[1] = to[...]
        elif k == 2:
            sums[0] += to[...]
            sums[1] -= to[...]
        else:
            sums[1] -= to[...]

    def middle(r, c):
        activate(1, r)
        activate(2, r)
        return c

    lax.fori_loop(0, RB + 2, middle, 0)

    def stage(i, sums, beside):
        for k in range(4):
            add_to(sums, k, product(i, k))
            for fn in beside[k]:
                fn()

    def later(fn, *args):
        return functools.partial(fn, *args)

    def all_inputs(i):
        return [later(inputs, i, k) for k in range(4)]

    def outer_work(i):
        rows = [later(activate, i, r) for r in range(RB + 2)]
        made = all_inputs(i)
        return rows[:3], rows[3:], made[:2], made[2:]

    inputs(1, 0)
    inputs(1, 1)
    ones, twos = all_inputs(1), all_inputs(2)
    stage(1, ysum.at[0], (ones[2:3], ones[3:] + twos[:1], twos[1:2], twos[2:]))
    stage(2, ysum.at[1], outer_work(0))
    for par in range(2):
        t1, t2 = ysum[0, par], ysum[1, par]
        ysum[0, par] = t1 + t2
        ysum[1, par] = t1 - t2

    def x3_slot(f, p):
        return f * 7 + p

    def d3_slot(f, p):
        return {0: 14, RB: 16}[p] + f if p in (0, RB) else f * 7 + RB + p - 1

    def halo_copy(f, up):
        return pltpu.make_async_remote_copy(
            src_ref=x1s.at[f, 1 if up else RB],
            dst_ref=x1s.at[f, RB + 1 if up else 0],
            send_sem=hsend_sem.at[f, 0 if up else 1],
            recv_sem=hrecv_sem.at[f, 0 if up else 1],
            device_id={"seg": s, "band": b - 1 if up else b + 1},
            device_id_type=MESH,
        )

    def finish(f, beside):
        stage(3 * f, rsum, beside)
        for par in range(2):
            y = ysum[f, par] + rsum[par] if f == 0 else ysum[f, par] - rsum[par]
            for tau in range(2):
                r = 1 + 2 * tau + par
                x1s[f, r] = (x0s[FR + f, r].astype(F32) + y[tau * COLS : (tau + 1) * COLS]).astype(BF)

    def send(f):
        pl.when(b > 0)(lambda: halo_copy(f, True).start())
        pl.when(b < BANDS - 1)(lambda: halo_copy(f, False).start())

    def receive(f):
        pl.when(b > 0)(lambda: halo_copy(f, False).wait_recv())
        pl.when(b < BANDS - 1)(lambda: halo_copy(f, True).wait_recv())

    def own_taps(f):
        rows = [x1s[f, 1 + p].astype(F32) for p in range(RB)]
        for p in range(RB):
            spread(x3_slot(f, p), rows[p])
            if p:
                spread(d3_slot(f, p), rows[p] - rows[p - 1])

    def edge_taps(f):
        above = jnp.where(b > 0, x1s[f, 0].astype(F32), 0.0)
        below = jnp.where(b < BANDS - 1, x1s[f, RB + 1].astype(F32), 0.0)
        spread(d3_slot(f, 0), x1s[f, 1].astype(F32) - above)
        spread(d3_slot(f, RB), below - x1s[f, RB].astype(F32))

    def phase(c2, m, slot, rows):
        x = taps[slot : slot + rows, :, c2 * C_MID : (c2 + 2) * C_MID].reshape(rows * COLS, 2 * C_MID)
        return lax.dot_general(x, u[c2 * 3 + m], (((1,), (1,)), ((), ())), preferred_element_type=F32)

    def place(f, r2, p0, y):
        full = (y[0][:, :128], y[0][:, 128:] + y[1][:, :128], y[1][:, 128:])
        for p in range(y[0].shape[0] // COLS):
            for l in range(3):
                at = pl.ds(2 * (p0 + p) + r2, COLS, stride=8)
                zs[f, l, at, :] = full[l][p * COLS : (p + 1) * COLS]

    def inner_rows(f):
        even, odd = [], []
        for c2 in range(2):
            mid = phase(c2, 0, x3_slot(f, 0), RB)
            even.append(mid[COLS:] + phase(c2, 1, d3_slot(f, 1), RB - 1))
            odd.append(mid[:-COLS] + phase(c2, 2, d3_slot(f, 1), RB - 1))
            prod[f, c2, :COLS, :256] = mid[:COLS]
            prod[f, c2, COLS:, :256] = mid[-COLS:]
        place(f, 0, 1, even)
        place(f, 1, 0, odd)

    def edge_rows():
        for e, (m, p, row) in enumerate(((1, 0, 0), (2, RB, RB - 1))):
            d = [phase(c2, m, d3_slot(0, p), FR) for c2 in range(2)]
            for f in range(FR):
                y = [prod[f, c2, e * COLS : (e + 1) * COLS, :256] + d[c2][f * COLS : (f + 1) * COLS] for c2 in range(2)]
                place(f, e, row, y)

    def pack(f):
        for q in range(COLS):
            for l in range(3):
                at = q * 2 * C_OUT + l * 128
                out[f, :, at : at + 128] = zs[f, l, q * 8 : (q + 1) * 8, :].astype(BF)

    finish(0, outer_work(3))
    send(0)
    finish(1, ([], [], [later(own_taps, 0)], []))
    send(1)
    own_taps(1)
    inner_rows(0)
    inner_rows(1)
    for f in range(FR):
        receive(f)
    for f in range(FR):
        edge_taps(f)
    edge_rows()
    for f in range(FR):
        pack(f)

    for f in range(FR):
        pl.when(b > 0)(lambda f=f: halo_copy(f, True).wait_send())
        pl.when(b < BANDS - 1)(lambda f=f: halo_copy(f, False).wait_send())
    each_latent_copy(lambda ds, tb, h: latent_copy(ds, tb, h).wait_send())
    for tb in range(BANDS):
        pl.when(b != tb)(lambda tb=tb: stat_copy(tb).wait_send())


def local(segs, latents, weight_in, weight_mid, weight_up, norm_gain, norm_shift):
    operands = (latents, weight_in, weight_mid, weight_up.T, norm_gain, norm_shift)
    return pl.pallas_call(
        functools.partial(decoder_kernel, segs),
        out_shape=pltpu.VMEM((FR, 2 * RB, 2 * COLS * C_OUT), BF),
        in_specs=[pl.BlockSpec(memory_space=pltpu.HBM)] * 6,
        out_specs=pl.BlockSpec(memory_space=pltpu.VMEM),
        scratch_shapes=[
            pltpu.VMEM((8, COLS * C_LAT), BF),
            pltpu.VMEM((C_MID,), F32),
            pltpu.VMEM((C_MID,), F32),
            pltpu.VMEM((3, 9 * C_LAT, C_MID), BF),
            pltpu.VMEM((C_OUT, 9 * C_MID), BF),
            pltpu.VMEM((4, QC, 128), BF),
            pltpu.VMEM((6, 4, QC, 128), BF),
            pltpu.VMEM((4 * COLS, 3 * 384), BF),
            pltpu.VMEM((3, 3 * 384, 2 * C_MID), BF),
            pltpu.VMEM((4, RB + 2, COLS, C_MID), BF),
            pltpu.VMEM((4, RB + 2, COLS, C_MID), BF),
            pltpu.VMEM((3, 9 * C_MID, C_MID), BF),
            pltpu.VMEM((len(MADE), TAPW, C_MID), BF),
            pltpu.VMEM((8, C_MID), F32),
            pltpu.VMEM((BANDS, 8, C_MID), F32),
            pltpu.VMEM((32, COLS, TAPW), BF),
            pltpu.VMEM((2, 2, 2 * COLS, C_MID), F32),
            pltpu.VMEM((FR, 2, 2 * COLS, C_MID), F32),
            pltpu.VMEM((2, 2 * COLS, C_MID), F32),
            pltpu.VMEM((FR, RB + 2, COLS, C_MID), BF),
            pltpu.VMEM((6, 256, 2 * C_MID), BF),
            pltpu.VMEM((FR, 3, COLS * 8, 128), F32),
            pltpu.SemaphoreType.DMA((6,)),
            pltpu.SemaphoreType.DMA((12,)),
            pltpu.SemaphoreType.DMA((12,)),
            pltpu.SemaphoreType.DMA((BANDS,)),
            pltpu.SemaphoreType.DMA((BANDS,)),
            pltpu.SemaphoreType.DMA((FR, 2)),
            pltpu.SemaphoreType.DMA((FR, 2)),
        ],
        compiler_params=pltpu.CompilerParams(collective_id=0, has_side_effects=True, vmem_limit_bytes=60 << 20),
        name="decoder",
    )(*(pltpu.with_memory_space_constraint(x, pltpu.HBM) for x in operands))


def solution(mesh):
    return jax.shard_map(
        functools.partial(local, mesh.shape["seg"]),
        mesh=mesh,
        in_specs=(P(("seg", "band"), None), P(), P(), P(), P(), P()),
        out_specs=P("seg", "band", None),
        check_vma=False,
    )
```
